128 devices in a mesh: grp: 2 (over z_hi), tx: 8 (over z_lo, x), ty: 8 (over y, core).
Axes of the slice: x: 4, y: 4, z: 4 (z_hi: 2, z_lo: 2; z = z_hi * 2 + z_lo), core: 2. Of those that a mesh axis runs over, the one named last changes fastest.
Arguments:
- velocity: float32 [3, 16, 1024, 2048], P(None, 'grp', 'tx', 'ty'), may hold values from -6 to 6
- viscosity: float32 [16, 1024, 2048], P('grp', 'tx', 'ty'), may hold values from 0.05 to 0.2
- mean_flow: float32 [16], replicated, may hold values from 0.3 to 1.5
- plane_pick: int32 [2], replicated, may hold values from 0 to 15
- embed_weight: bfloat16 [768, 1024], replicated, may hold values from -0.21875 to 0.21875
- norm_gain: float32 [1024], replicated, may hold values from 0.5 to 1.5
- project_weight: bfloat16 [1024, 3072], replicated, may hold values from -8 to 8
- output_weight: bfloat16 [1024, 1024], replicated, may hold values from -0.1875 to 0.1875
- cotangent: bfloat16 [2, 64, 128, 1024], P('grp', 'tx', 'ty'), may hold values from -0.059814453 to 0.059814453
Outputs:
- new_velocity: float32 [3, 16, 1024, 2048], P(None, 'grp', 'tx', 'ty')
- grad_project: float32 [1024, 3072], P(('grp', 'tx', 'ty'))
- grad_output: float32 [1024, 1024], P(('grp', 'tx', 'ty'))
- grad_gain: float32 [1024], P(('grp', 'tx', 'ty'))
The draws below stay inside these ranges and needn't reach their ends.
Inputs may be any that keep to these rules, and one draw needn't show every extreme that they name: `plane_pick`: each sample's plane index.
All inputs are finite; a program needn't handle non-finite values.
Results may differ from the reference program's by a relative error of at most 0.025.
Values may be sent and summed in bfloat16 or wider, within the bound.
No kernel may reach another device: no remote copies, remote signals or barrier semaphores. Data moves between devices by JAX's collectives and lax.ppermute only.
A program may use at most 128 MiB of HBM per device.

```python
import math
import jax
import jax.numpy as jnp
from jax import lax

D = 1024
HEADS = 16
PATCH = 16
CHANNELS = 3
HEAD_DIM = 64
PDIM = 768
PLANES = 16
NX = 1024
NY = 2048
PNX = 64
PNY = 128
SAMPLES = 2


def draw_project_weight(key, part):
    drawn = jax.random.normal(key, (D, 3 * D), jnp.float32) * D ** (-0.5)
    return jnp.clip(drawn, -8.0, 8.0).astype(jnp.bfloat16)


def level_of(rng, extent, shards, least, largest):
    gain = 1.0
    for dim, parts in shards:
        steps = jax.random.uniform(jax.random.fold_in(jax.random.fold_in(rng, 6), dim), (parts,), jnp.float32, least / len(shards), largest / len(shards))
        gain = gain * jnp.repeat(jnp.exp(steps), extent[dim] // parts).reshape((-1,) + (1,) * (len(extent) - 1 - dim))
    return gain


def bell_draw(rng, extent, scale, reach, cuts=(), dtype=jnp.bfloat16):
    values = jax.random.normal(rng, extent, jnp.float32) * scale
    if len(cuts) > 0:
        values = level_of(rng, extent, cuts, -0.22, 0.18) * values
    return jnp.clip(values, min=-reach, max=reach).astype(dtype)


def setup_inputs(seed: int = 0) -> dict:
    key_of = jax.random.split(jax.random.key(seed), 10)
    return {
        "velocity": bell_draw(key_of[0], (CHANNELS, PLANES, NX, NY), 1.0, 6.0, ((1, 2), (2, 8), (3, 8)), jnp.float32),
        "viscosity": jnp.clip(jnp.exp(math.log(0.2) - 1.3862944 * jax.random.uniform(key_of[1], (PLANES, NX, NY), jnp.float32) ** level_of(key_of[1], (PLANES, NX, NY), ((0, 2), (1, 8), (2, 8)), -0.2, 0.2)), 0.05, 0.2),
        "mean_flow": jnp.clip(jax.random.uniform(key_of[2], (PLANES,), jnp.float32, 0.3, 1.5), 0.3, 1.5),
        "plane_pick": jax.random.randint(key_of[3], (SAMPLES,), 0, PLANES).astype(jnp.int32),
        "embed_weight": bell_draw(key_of[4], (PDIM, D), PDIM ** -0.5, 0.21875),
        "norm_gain": jnp.clip(1.0 + 0.1 * jax.random.normal(key_of[5], (D,), jnp.float32), 0.5, 1.5),
        "project_weight": draw_project_weight(jax.random.fold_in(key_of[9], 71), 0),
        "output_weight": bell_draw(key_of[7], (D, D), D ** -0.5, 0.1875),
        "cotangent": bell_draw(key_of[8], (SAMPLES, PNX, PNY, D), 0.01, 0.059814453, ((0, 2), (1, 8), (2, 8))),
    }


time_step = 0.5
norm_eps = 1e-06

def advance(current, viscous, flow_rows):
    centre = current[:, 1:-1, 1:-1, 1:-1]
    interior = viscous[1:-1, 1:-1, 1:-1]
    onward_x = current[:, 1:-1, 2:, 1:-1]
    behind_x = current[:, 1:-1, :-2, 1:-1]
    neighbours = ((current[:, 2:, 1:-1, 1:-1], current[:, :-2, 1:-1, 1:-1], viscous[2:, 1:-1, 1:-1], viscous[:-2, 1:-1, 1:-1]), (onward_x, behind_x, viscous[1:-1, 2:, 1:-1], viscous[1:-1, :-2, 1:-1]), (current[:, 1:-1, 1:-1, 2:], current[:, 1:-1, 1:-1, :-2], viscous[1:-1, 1:-1, 2:], viscous[1:-1, 1:-1, :-2]))
    diffusion = jnp.zeros_like(centre)
    for onward, behind, visc_onward, visc_behind in neighbours:
        diffusion = diffusion + 0.5 * (interior + visc_onward) * (onward - centre) - 0.5 * (interior + visc_behind) * (centre - behind)
    transport = flow_rows[:, None, None] * 0.5 * (onward_x - behind_x)
    return centre + time_step * (diffusion - transport)

def pad_both(current, viscous):
    padded = jnp.pad(current, ((0, 0), (1, 1), (0, 0), (0, 0)))
    padded = jnp.pad(padded, ((0, 0), (0, 0), (1, 1), (1, 1)), mode='wrap')
    visc_pad = jnp.pad(viscous, ((1, 1), (0, 0), (0, 0)))
    visc_pad = jnp.pad(visc_pad, ((0, 0), (1, 1), (1, 1)), mode='wrap')
    return (padded, visc_pad)

def patchify(plane):
    extent_x = plane.shape[1] // PATCH
    extent_y = plane.shape[2] // PATCH
    blocks = plane.reshape(CHANNELS, extent_x, PATCH, extent_y, PATCH)
    return blocks.transpose(1, 3, 0, 2, 4).reshape(extent_x, extent_y, PDIM)

def line_probs(query_rows, key_rows):
    scores = jnp.einsum('qbhd,kbhd->bhqk', query_rows.astype(jnp.float32), key_rows.astype(jnp.float32)) * HEAD_DIM ** (-0.5)
    scores = scores - lax.optimization_barrier(jnp.max(scores, axis=-1, keepdims=True))
    expsum = jnp.exp(scores)
    return expsum / lax.optimization_barrier(jnp.sum(expsum, axis=-1, keepdims=True))

def line_pass(query_rows, key_rows, value_rows, grad_rows):
    probs = line_probs(query_rows, key_rows)
    weights = probs.astype(jnp.bfloat16).astype(jnp.float32)
    value_wide = value_rows.astype(jnp.float32)
    grad_wide = grad_rows.astype(jnp.float32)
    attended = jnp.einsum('bhqk,kbhd->qbhd', weights, value_wide).astype(jnp.bfloat16)
    dprob = jnp.einsum('qbhd,kbhd->bhqk', grad_wide, value_wide)
    delta = lax.optimization_barrier(jnp.sum(probs * dprob, axis=-1, keepdims=True))
    dscore = (probs * (dprob - delta) * HEAD_DIM ** (-0.5)).astype(jnp.bfloat16).astype(jnp.float32)
    dquery = jnp.einsum('bhqk,kbhd->qbhd', dscore, key_rows.astype(jnp.float32)).astype(jnp.bfloat16)
    dkey = jnp.einsum('bhqk,qbhd->kbhd', dscore, query_rows.astype(jnp.float32)).astype(jnp.bfloat16)
    dvalue = jnp.einsum('bhqk,qbhd->kbhd', weights, grad_wide).astype(jnp.bfloat16)
    return (attended, dquery, dkey, dvalue)

def reference(velocity, viscosity, mean_flow, plane_pick, embed_weight, norm_gain, project_weight, output_weight, cotangent):
    current = velocity
    for substep_turn in range(2):
        padded, visc_pad = pad_both(current, viscosity)
        current = advance(padded, visc_pad, mean_flow)
    sample_plane = jnp.take(current, plane_pick, axis=1).transpose(1, 0, 2, 3).astype(jnp.bfloat16)
    split_at = HEADS // 2

    def sample_pass(operands):
        plane, sample_grad = operands
        token_rows = patchify(plane).reshape(-1, PDIM)
        embedded = jnp.dot(token_rows, embed_weight, preferred_element_type=jnp.float32).astype(jnp.bfloat16)
        widened = embedded.astype(jnp.float32)
        centred = widened - lax.optimization_barrier(jnp.mean(widened, axis=-1, keepdims=True))
        unit = centred * lax.rsqrt(lax.optimization_barrier(jnp.mean(centred * centred, axis=-1, keepdims=True)) + norm_eps)
        normed = (unit * norm_gain).astype(jnp.bfloat16)
        projected = jnp.dot(normed, project_weight, preferred_element_type=jnp.float32).astype(jnp.bfloat16)
        grad_tokens = sample_grad.reshape(-1, D)
        back = jnp.dot(grad_tokens, output_weight.T, preferred_element_type=jnp.float32).astype(jnp.bfloat16)

        def heads(columns):
            return columns.reshape(PNX, PNY, HEADS, HEAD_DIM)
        query_heads = heads(projected[:, :D])
        key_heads = heads(projected[:, D:2 * D])
        value_heads = heads(projected[:, 2 * D:])
        grad_heads = heads(back)
        first = line_pass(query_heads[:, :, :split_at], key_heads[:, :, :split_at], value_heads[:, :, :split_at], grad_heads[:, :, :split_at])
        second = line_pass(query_heads[:, :, split_at:].transpose(1, 0, 2, 3), key_heads[:, :, split_at:].transpose(1, 0, 2, 3), value_heads[:, :, split_at:].transpose(1, 0, 2, 3), grad_heads[:, :, split_at:].transpose(1, 0, 2, 3))
        second = tuple((operand.transpose(1, 0, 2, 3) for operand in second))
        merged = [jnp.concatenate([first[member], second[member]], axis=2).reshape(-1, D) for member in range(4)]
        attended, dquery, dkey, dvalue = merged
        dprojected = jnp.concatenate([dquery, dkey, dvalue], axis=1)
        grad_output = jnp.dot(attended.T, grad_tokens, preferred_element_type=jnp.float32)
        grad_project = jnp.dot(normed.T, dprojected, preferred_element_type=jnp.float32)
        dnormed = jnp.dot(dprojected, project_weight.T, preferred_element_type=jnp.float32)
        grad_gain = lax.optimization_barrier(jnp.sum(dnormed * unit, axis=0))
        return (grad_project, grad_output, grad_gain)
    grad_project, grad_output, grad_gain = lax.map(sample_pass, (sample_plane, cotangent))
    return (current, lax.optimization_barrier(jnp.sum(grad_project, axis=0)), lax.optimization_barrier(jnp.sum(grad_output, axis=0)), lax.optimization_barrier(jnp.sum(grad_gain, axis=0)))
```

```python
import functools

import jax
import jax.numpy as jnp
from jax import lax
from jax.experimental import pallas as pl
from jax.experimental.pallas import tpu as pltpu
from jax.sharding import PartitionSpec as P

D = 1024
HEADS = 16
PATCH = 16
CHANNELS = 3
HEAD_DIM = 64
PDIM = 768
DEPTH = 8
ROWS = 128
COLS = 256
NORM_EPS = 1e-06
F32 = jnp.float32
BF16 = jnp.bfloat16


TOP = 16
TALL = 160


def shift(count, step):
    return [(i, (i + step) % count) for i in range(count)]


def diagonal(step):
    return [(g * 8 + t, (1 - g) * 8 + (t + step) % 8) for g in range(2) for t in range(8)]


SWAP = [(0, 1), (1, 0)]


def lane_ids(rows):
    return lax.broadcasted_iota(jnp.int32, (rows, 128), 1)


def next_lane(tile, after, lane):
    return jnp.where(lane == 127, pltpu.roll(after, 127, 1), pltpu.roll(tile, 127, 1))


def previous_lane(tile, before, lane):
    return jnp.where(lane == 0, pltpu.roll(before, 1, 1), pltpu.roll(tile, 1, 1))


def substep_block(cells, plane, viscous, vplane, tile, row, rows, flow, lane):
    after, before = (tile + 1) % 3, (tile + 2) % 3
    here = viscous(vplane, tile, row)
    sides = (
        viscous(vplane + 1, tile, row),
        viscous(vplane - 1, tile, row),
        viscous(vplane, tile, row + 1),
        viscous(vplane, tile, row - 1),
        next_lane(here, viscous(vplane, after, row), lane),
        previous_lane(here, viscous(vplane, before, row), lane),
    )
    faces = [here + s for s in sides]
    keep = 1.0 - (faces[0] + faces[1] + faces[2] + faces[3] + faces[4] + faces[5])
    faces[2] = faces[2] - flow
    faces[3] = faces[3] + flow
    results = []
    for f in range(CHANNELS):
        centre = cells(f, plane, tile, row)
        total = keep * centre
        total = total + faces[0] * cells(f, plane + 1, tile, row)
        total = total + faces[1] * cells(f, plane - 1, tile, row)
        total = total + faces[2] * cells(f, plane, tile, row + 1)
        total = total + faces[3] * cells(f, plane, tile, row - 1)
        total = total + faces[4] * next_lane(centre, cells(f, plane, after, row), lane)
        total = total + faces[5] * previous_lane(centre, cells(f, plane, before, row), lane)
        results.append(total)
    return results


def stencil_kernel(
    where_ref, flow_ref, vel_ref, visc_ref, zhalo_ref, xlow_ref, xhigh_ref, yedge_ref, zxlow_ref, zxhigh_ref,
    zyedge_ref, new_ref, chosen_ref, pad_ref, half_ref,
):
    group = where_ref[0]
    first = group == 0
    spread_row = lax.broadcasted_iota(jnp.int32, (8, 128), 0)
    spread_lane = lax.broadcasted_iota(jnp.int32, (8, 128), 1)
    spread = (
        ((spread_row == 0) & (spread_lane == 0))
        | ((spread_row == 1) & (spread_lane == 1))
        | ((spread_row == 2) & (spread_lane == 126))
        | ((spread_row == 3) & (spread_lane == 127))
    ).astype(F32)

    def edge(block):
        return lax.dot_general(block.astype(F32), spread, (((0,), (0,)), ((), ())), preferred_element_type=F32)

    def load_plane(z, carry):
        for f in range(4):
            scale = 1.0 if f < CHANNELS else 0.25
            source = vel_ref[f, z] if f < CHANNELS else visc_ref[z] * scale
            low = xlow_ref[f, z].astype(F32) * scale
            high = xhigh_ref[f, z].astype(F32) * scale
            for t in range(2):
                lanes = slice(128 * t, 128 * t + 128)
                pad_ref[f, z + 2, t, TOP : TOP + ROWS, :] = source[:, lanes]
                pad_ref[f, z + 2, t, TOP - 2 : TOP, :] = low[:, lanes]
                pad_ref[f, z + 2, t, TOP + ROWS : TOP + ROWS + 2, :] = high[:, lanes]
            edges = yedge_ref[f, z]
            pad_ref[f, z + 2, 2, TOP : TOP + ROWS, :] = edge(edges[:, :128]) * scale
            corner = edge(edges[:, 128:]) * scale
            pad_ref[f, z + 2, 2, TOP - 1 : TOP, :] = corner[0:1]
            pad_ref[f, z + 2, 2, TOP + ROWS : TOP + ROWS + 1, :] = corner[1:2]
        return carry

    lax.fori_loop(0, DEPTH, load_plane, 0)
    base = jnp.where(first, 10, 0)
    near = jnp.where(first, 10, 1)
    zero = jnp.zeros((TALL, 128), F32)
    for f in range(4):
        scale = 1.0 if f < CHANNELS else 0.25
        for j in range(2):
            for t in range(3):
                pad_ref[f, 10 - base + j, t] = zero
            for t in range(2):
                pad_ref[f, base + j, t, TOP : TOP + ROWS, :] = (
                    zhalo_ref[f, j, :, 128 * t : 128 * t + 128].astype(F32) * scale
                )
        for t in range(2):
            lanes = slice(128 * t, 128 * t + 128)
            pad_ref[f, near, t, TOP - 1 : TOP, :] = zxlow_ref[f, :, lanes].astype(F32) * scale
            pad_ref[f, near, t, TOP + ROWS : TOP + ROWS + 1, :] = zxhigh_ref[f, :, lanes].astype(F32) * scale
        pad_ref[f, near, 2, TOP : TOP + ROWS, :] = edge(zyedge_ref[f]) * scale

    def first_pass(step, carry):
        at = step + jnp.where(first, 1, 0)
        flow = 0.25 * flow_ref[group * DEPTH + at]
        rows = 24
        lane = lane_ids(rows)
        cells = lambda f, z, t, r: pad_ref[f, z, t, r : r + rows, :]
        viscous = lambda z, t, r: pad_ref[3, z, t, r : r + rows, :]
        for t in range(3):
            for block in range(6):
                r = 8 + rows * block
                done = substep_block(cells, at + 1, viscous, at + 1, t, r, rows, flow, lane)
                for f in range(CHANNELS):
                    half_ref[f, at, t, r : r + rows, :] = done[f]
        return carry

    lax.fori_loop(0, 9, first_pass, 0)
    wall = jnp.where(first, 0, 9)
    for f in range(CHANNELS):
        for t in range(3):
            half_ref[f, wall, t] = zero

    def second_pass(z, carry):
        flow = 0.25 * flow_ref[group * DEPTH + z + 1]
        rows = 32
        lane = lane_ids(rows)
        cells = lambda f, p, t, r: half_ref[f, p, t, r : r + rows, :]
        viscous = lambda p, t, r: pad_ref[3, p, t, r : r + rows, :]
        for t in range(2):
            for block in range(4):
                r = TOP + rows * block
                done = substep_block(cells, z + 1, viscous, z + 2, t, r, rows, flow, lane)
                for f in range(CHANNELS):
                    new_ref[f, z, rows * block : rows * block + rows, 128 * t : 128 * t + 128] = done[f]
        return carry

    lax.fori_loop(0, DEPTH, second_pass, 0)
    for s in range(2):
        local = where_ref[1 + s] - group * DEPTH
        inside = (local >= 0) & (local < DEPTH)
        safe = jnp.clip(local, 0, DEPTH - 1)
        for f in range(CHANNELS):
            chosen_ref[s, f] = jnp.where(inside, new_ref[f, safe], 0.0).astype(BF16)


def stencil(where, flow, velocity, viscosity, zhalo, xlow, xhigh, yedge, zxlow, zxhigh, zyedge):
    vmem = pl.BlockSpec(memory_space=pltpu.VMEM)
    smem = pl.BlockSpec(memory_space=pltpu.SMEM)
    return pl.pallas_call(
        stencil_kernel,
        out_shape=(
            jax.ShapeDtypeStruct((CHANNELS, DEPTH, ROWS, COLS), F32),
            jax.ShapeDtypeStruct((2, CHANNELS, ROWS, COLS), BF16),
        ),
        in_specs=[smem, smem] + [vmem] * 9,
        out_specs=(vmem, vmem),
        scratch_shapes=[
            pltpu.VMEM((4, 12, 3, TALL, 128), F32),
            pltpu.VMEM((CHANNELS, 10, 3, TALL, 128), F32),
        ],
        compiler_params=pltpu.CompilerParams(vmem_limit_bytes=48 * 1024 * 1024),
        name="stencil",
    )(where, flow, velocity, viscosity, zhalo, xlow, xhigh, yedge, zxlow, zxhigh, zyedge)


def layer_kernel(along_rows, *refs):
    token_refs, cot_refs = refs[:8], refs[8:16]
    embed_ref, gain_ref, weight_ref, back_ref, out_ref = refs[16:21]
    tokens, cots, normed, qk, vg = refs[21:]
    for c in range(8):
        tokens[c] = token_refs[c][...]
        cots[128 * c : 128 * c + 128, :] = cot_refs[c][...]

    def project(c, carry):
        at = pl.multiple_of(c * 128, 128)
        embedded = jnp.dot(tokens[c], embed_ref[...], preferred_element_type=F32).astype(BF16).astype(F32)
        centred = embedded - jnp.mean(embedded, axis=-1, keepdims=True)
        unit = centred * lax.rsqrt(jnp.mean(centred * centred, axis=-1, keepdims=True) + NORM_EPS)
        rows = (unit * gain_ref[...]).astype(BF16)
        normed[pl.ds(at, 128), :] = rows
        projected = jnp.dot(rows, weight_ref[...], preferred_element_type=F32).astype(BF16).astype(F32)
        back = lax.dot_general(
            cots[pl.ds(at, 128), :], back_ref[...], (((1,), (1,)), ((), ())), preferred_element_type=F32
        ).astype(BF16).astype(F32)
        qk[pl.ds(at, 128), :] = projected[:, :128]
        vg[pl.ds(at, 128), :] = projected[:, 128:] + back
        return carry

    lax.fori_loop(0, 8, project, 0)
    lane = lane_ids(128)
    low = lane < 64
    rowline = lax.broadcasted_iota(jnp.int32, (128, 128), 0) // 64
    same = rowline == lane // 64
    for p in range(8):
        if along_rows:
            load = lambda ref: jnp.concatenate([ref[2 * p : 1024 : 16, :], ref[2 * p + 1 : 1024 : 16, :]], axis=0)
        else:
            load = lambda ref: jnp.concatenate(
                [ref[128 * c + 16 * p : 128 * c + 16 * p + 16, :] for c in range(8)], axis=0
            )
        qk_wide, vg_wide = load(qk), load(vg)
        kq_wide, gv_wide = pltpu.roll(qk_wide, 64, 1), pltpu.roll(vg_wide, 64, 1)
        only_low = lambda a: jnp.where(low, a, 0.0).astype(BF16)
        only_high = lambda a: jnp.where(low, 0.0, a).astype(BF16)
        nt = (((1,), (1,)), ((), ()))
        tn = (((0,), (0,)), ((), ()))
        scores = lax.dot_general(only_low(qk_wide), kq_wide.astype(BF16), nt, preferred_element_type=F32)
        scores = scores * HEAD_DIM**-0.5
        if along_rows:
            scores = jnp.where(same, scores, -1e30)
        raised = jnp.exp(scores - jnp.max(scores, axis=-1, keepdims=True))
        probs = raised / jnp.sum(raised, axis=-1, keepdims=True)
        weights = probs.astype(BF16)
        dprob = lax.dot_general(only_low(gv_wide), vg_wide.astype(BF16), nt, preferred_element_type=F32)
        delta = jnp.sum(probs * dprob, axis=-1, keepdims=True)
        dscore = (probs * (dprob - delta) * HEAD_DIM**-0.5).astype(BF16)
        dqk = jnp.dot(dscore, only_low(kq_wide), preferred_element_type=F32) + lax.dot_general(
            dscore, only_high(kq_wide), tn, preferred_element_type=F32
        )
        dva = lax.dot_general(weights, only_low(gv_wide), tn, preferred_element_type=F32) + jnp.dot(
            weights, only_high(gv_wide), preferred_element_type=F32
        )
        for ref, value in ((qk, dqk), (vg, dva)):
            if along_rows:
                ref[2 * p : 1024 : 16, :] = value[:64]
                ref[2 * p + 1 : 1024 : 16, :] = value[64:]
            else:
                for c in range(8):
                    ref[128 * c + 16 * p : 128 * c + 16 * p + 16, :] = value[16 * c : 16 * c + 16]
    dqk, dva = qk[...].astype(BF16), vg[...].astype(BF16)
    tn = (((0,), (0,)), ((), ()))
    grad_output = lax.dot_general(dva, cots[...], tn, preferred_element_type=F32)[64:]
    low64 = lane_ids(64) < 64
    out_ref[:, :128] = lax.dot_general(normed[...], dqk, tn, preferred_element_type=F32).astype(BF16)
    values = lax.dot_general(normed[...], dva, tn, preferred_element_type=F32)
    for c in range(16):
        piece = grad_output[:, 128 * (c // 2) : 128 * (c // 2) + 128]
        if c % 2 == 0:
            piece = pltpu.roll(piece, 64, 1)
        out_ref[64 * c : 64 * c + 64, 128:] = jnp.where(low64, values[64 * c : 64 * c + 64], piece).astype(BF16)


def layer(along_rows, tokens, cots, embed_weight, gain, weight, back):
    vmem = pl.BlockSpec(memory_space=pltpu.VMEM)
    return pl.pallas_call(
        functools.partial(layer_kernel, along_rows),
        out_shape=jax.ShapeDtypeStruct((D, 256), BF16),
        in_specs=[vmem] * 20,
        out_specs=vmem,
        scratch_shapes=[
            pltpu.VMEM((8, 128, PDIM), BF16),
            pltpu.VMEM((1024, D), BF16),
            pltpu.VMEM((1024, D), BF16),
            pltpu.VMEM((1024, 128), F32),
            pltpu.VMEM((1024, 128), F32),
        ],
        compiler_params=pltpu.CompilerParams(vmem_limit_bytes=48 * 1024 * 1024),
        name="layer_rows" if along_rows else "layer_columns",
    )(*tokens, *cots, embed_weight, gain, weight, back)


def patchify(plane):
    blocks = plane.reshape(CHANNELS, ROWS // PATCH, PATCH, COLS // PATCH, PATCH)
    return blocks.transpose(1, 3, 0, 2, 4).reshape(128, PDIM)


def gather_rows(mine):
    within = lambda k: [(i, (i // 4) * 4 + (i + k) % 4) for i in range(8)]
    across = [(i, i ^ 4) for i in range(8)]
    other = lax.ppermute(mine, "tx", across)
    return [mine, other] + [lax.ppermute(a, "tx", within(k)) for k in (1, 2, 3) for a in (mine, other)]


def gather_columns(mine):
    partner = [(i, i ^ 1) for i in range(8)]
    chunks = [mine] + [lax.ppermute(mine, "ty", shift(8, k)) for k in (2, 4, 6)]
    return chunks + [lax.ppermute(a, "ty", partner) for a in chunks]


def head_weights(project_weight, output_weight, head):
    parts = [lax.dynamic_slice_in_dim(project_weight, part * D + head * HEAD_DIM, HEAD_DIM, 1) for part in range(3)]
    weight = jnp.concatenate(parts + [jnp.zeros((D, HEAD_DIM), BF16)], axis=1)
    back = lax.dynamic_slice_in_dim(output_weight, head * HEAD_DIM, HEAD_DIM, 0)
    return weight, jnp.concatenate([jnp.zeros((HEAD_DIM, D), BF16), back], axis=0)


def shards(
    velocity, viscosity, mean_flow, plane_pick, embed_weight, norm_gain, project_weight, output_weight, cotangent
):
    group, row, column = lax.axis_index("grp"), lax.axis_index("tx"), lax.axis_index("ty")

    def planes(begin, count):
        cut = [
            lax.dynamic_slice_in_dim(velocity, begin, count, 1),
            lax.dynamic_slice_in_dim(viscosity, begin, count, 0)[None],
        ]
        return jnp.concatenate(cut, axis=0).astype(BF16)

    def cells(rows, columns):
        cut = [velocity[:, :, rows, columns], viscosity[None, :, rows, columns]]
        return jnp.concatenate(cut, axis=0).astype(BF16)

    every = slice(None)
    zhalo = lax.ppermute(planes((1 - group) * (DEPTH - 2), 2), "grp", SWAP)
    xlow = lax.ppermute(cells(slice(ROWS - 2, ROWS), every), "tx", shift(8, 1))
    xhigh = lax.ppermute(cells(slice(0, 2), every), "tx", shift(8, -1))
    facing = planes((1 - group) * (DEPTH - 1), 1)[:, 0]
    zxlow = lax.ppermute(facing[:, ROWS - 1 : ROWS, :], ("grp", "tx"), diagonal(1))
    zxhigh = lax.ppermute(facing[:, 0:1, :], ("grp", "tx"), diagonal(-1))
    zylow = lax.ppermute(facing[:, :, COLS - 1], ("grp", "ty"), diagonal(1))
    zyhigh = lax.ppermute(facing[:, :, 0], ("grp", "ty"), diagonal(-1))

    def side(columns):
        parts = [cells(every, columns), xlow[:, :, 1:2, columns], xhigh[:, :, 0:1, columns]]
        return jnp.concatenate([a.transpose(0, 1, 3, 2) for a in parts], axis=3)

    ylow = lax.ppermute(side(slice(COLS - 2, COLS)), "ty", shift(8, 1))
    yhigh = lax.ppermute(side(slice(0, 2)), "ty", shift(8, -1))
    yedge = jnp.pad(jnp.concatenate([yhigh, ylow], axis=2), ((0, 0), (0, 0), (0, 4), (0, 126)))
    nothing = jnp.zeros_like(zylow)
    zyedge = jnp.stack([zyhigh, nothing, nothing, zylow] + [nothing] * 4, axis=1)
    where = jnp.concatenate([group[None].astype(jnp.int32), plane_pick])
    new_velocity, chosen = stencil(
        where, jnp.pad(mean_flow, 1), velocity, viscosity, zhalo, xlow, xhigh, yedge, zxlow, zxhigh, zyedge
    )

    kept = lax.dynamic_index_in_dim(chosen, group, 0, keepdims=False)
    sent = lax.dynamic_index_in_dim(chosen, 1 - group, 0, keepdims=False)
    plane = kept + lax.ppermute(sent, "grp", SWAP)
    tokens = patchify(plane)
    cots = cotangent.reshape(128, D)
    gain = norm_gain[None]
    outs = []
    for along_rows, head in ((True, row), (False, 8 + column)):
        gather = gather_rows if along_rows else gather_columns
        weight, back = head_weights(project_weight, output_weight, head)
        outs.append(layer(along_rows, gather(tokens), gather(cots), embed_weight, gain, weight, back))
    partial = jnp.concatenate(outs, axis=1).reshape(128, 8, 512)
    arrived = lax.all_to_all(partial, ("grp", "tx", "ty"), split_axis=0, concat_axis=0, tiled=True)
    arrived = arrived.reshape(2, 8, 8, 8, 512).astype(F32)
    heads = jnp.concatenate(
        [jnp.sum(arrived[..., :256], axis=(0, 2)), jnp.sum(arrived[..., 256:], axis=(0, 1))], axis=0
    )
    grad_project = heads[..., :192].reshape(HEADS, 8, 3, HEAD_DIM).transpose(1, 2, 0, 3).reshape(8, 3 * D)
    pieces = lax.all_to_all(heads[..., 192:], ("grp", "tx"), split_axis=0, concat_axis=0, tiled=True)
    grad_output = pieces.transpose(1, 0, 2).reshape(8, D)
    first_row = ((group * 8 + row) * 8 + column) * 8
    weight_rows = lax.dynamic_slice_in_dim(project_weight, first_row, 8, 0).astype(F32)
    gains = lax.dynamic_slice_in_dim(norm_gain, first_row, 8, 0)
    grad_gain = jnp.sum(weight_rows * grad_project, axis=1) / gains
    return new_velocity, grad_project, grad_output, grad_gain


def solution(mesh):
    in_specs = (
        P(None, "grp", "tx", "ty"),
        P("grp", "tx", "ty"),
        P(),
        P(),
        P(),
        P(),
        P(),
        P(),
        P("grp", "tx", "ty", None),
    )
    out_specs = (
        P(None, "grp", "tx", "ty"),
        P(("grp", "tx", "ty"), None),
        P(("grp", "tx", "ty"), None),
        P(("grp", "tx", "ty")),
    )
    return jax.shard_map(shards, mesh=mesh, in_specs=in_specs, out_specs=out_specs, check_vma=False)
```

```python
import functools

import jax
import jax.numpy as jnp
from jax import lax
from jax.experimental import pallas as pl
from jax.experimental.pallas import tpu as pltpu
from jax.sharding import PartitionSpec as P

D = 1024
HEADS = 16
PATCH = 16
CHANNELS = 3
HEAD_DIM = 64
PDIM = 768
DEPTH = 8
ROWS = 128
COLS = 256
NORM_EPS = 1e-06
F32 = jnp.float32
BF16 = jnp.bfloat16


TOP = 16
TALL = 160


def shift(count, step):
    return [(i, (i + step) % count) for i in range(count)]


SWAP = [(0, 1), (1, 0)]


def lane_ids(rows):
    return lax.broadcasted_iota(jnp.int32, (rows, 128), 1)


def next_lane(tile, after, lane):
    return jnp.where(lane == 127, pltpu.roll(after, 127, 1), pltpu.roll(tile, 127, 1))


def previous_lane(tile, before, lane):
    return jnp.where(lane == 0, pltpu.roll(before, 1, 1), pltpu.roll(tile, 1, 1))


def substep_block(cells, plane, viscous, vplane, tile, row, rows, flow, lane):
    after, before = (tile + 1) % 3, (tile + 2) % 3
    here = viscous(vplane, tile, row)
    sides = (
        viscous(vplane + 1, tile, row),
        viscous(vplane - 1, tile, row),
        viscous(vplane, tile, row + 1),
        viscous(vplane, tile, row - 1),
        next_lane(here, viscous(vplane, after, row), lane),
        previous_lane(here, viscous(vplane, before, row), lane),
    )
    faces = [here + s for s in sides]
    keep = 1.0 - (faces[0] + faces[1] + faces[2] + faces[3] + faces[4] + faces[5])
    faces[2] = faces[2] - flow
    faces[3] = faces[3] + flow
    results = []
    for f in range(CHANNELS):
        centre = cells(f, plane, tile, row)
        total = keep * centre
        total = total + faces[0] * cells(f, plane + 1, tile, row)
        total = total + faces[1] * cells(f, plane - 1, tile, row)
        total = total + faces[2] * cells(f, plane, tile, row + 1)
        total = total + faces[3] * cells(f, plane, tile, row - 1)
        total = total + faces[4] * next_lane(centre, cells(f, plane, after, row), lane)
        total = total + faces[5] * previous_lane(centre, cells(f, plane, before, row), lane)
        results.append(total)
    return results


def edge_tile(packed, k, lane):
    after = pltpu.roll(packed, lax.rem(128 - 2 * k, 128), 1)
    before = pltpu.roll(packed, lax.rem(190 - 2 * k, 128), 1)
    return jnp.where(lane < 2, after, jnp.where(lane >= 126, before, 0.0))


class Block:
    def __init__(self, where_ref, vel_ref, visc_ref, zhalo_ref, xlow_ref, xhigh_ref, packed_ref, zedge_ref):
        self.group = where_ref[0]
        self.first = self.group == 0
        self.vel, self.visc, self.zhalo, self.xlow, self.xhigh = vel_ref, visc_ref, zhalo_ref, xlow_ref, xhigh_ref
        self.packed, self.zedge = packed_ref, zedge_ref

    def fill_own(self, pad_ref, slot, z):
        packed = self.packed[...].astype(F32)
        lane = lane_ids(TALL)
        for f in range(4):
            scale = 1.0 if f < CHANNELS else 0.25
            source = self.vel[f, z] if f < CHANNELS else self.visc[z] * scale
            low = self.xlow[f, z].astype(F32) * scale
            high = self.xhigh[f, z].astype(F32) * scale
            for t in range(2):
                lanes = slice(128 * t, 128 * t + 128)
                pad_ref[f, slot, t, TOP : TOP + ROWS, :] = source[:, lanes]
                pad_ref[f, slot, t, TOP - 2 : TOP, :] = low[:, lanes]
                pad_ref[f, slot, t, TOP + ROWS : TOP + ROWS + 2, :] = high[:, lanes]
            pad_ref[f, slot, 2] = edge_tile(packed, f * DEPTH + z, lane) * scale

    def fill_halo(self, pad_ref, slot, j):
        packed = self.zedge[:TALL].astype(F32)
        edges = self.zedge[TALL:].astype(F32)
        lane = lane_ids(TALL)
        facing = jnp.where(self.first, 0, DEPTH - 1)
        for f in range(4):
            scale = 1.0 if f < CHANNELS else 0.25
            for t in range(2):
                lanes = slice(128 * t, 128 * t + 128)
                at = 2 * f + t
                pad_ref[f, slot, t, TOP : TOP + ROWS, :] = self.zhalo[f, j, :, lanes].astype(F32) * scale
                pad_ref[f, slot, t, TOP - 1 : TOP, :] = edges[at : at + 1] * scale
                pad_ref[f, slot, t, TOP + ROWS : TOP + ROWS + 1, :] = edges[8 + at : 9 + at] * scale
            pad_ref[f, slot, 2] = edge_tile(packed, f * DEPTH + facing, lane) * scale

    def fill_zero(self, pad_ref, slot):
        for f in range(pad_ref.shape[0]):
            for t in range(3):
                pad_ref[f, slot, t] = jnp.zeros((TALL, 128), F32)


def first_pass(pad_ref, half_ref, slot, flow):
    rows = 24
    lane = lane_ids(rows)
    cells = lambda f, z, t, r: pad_ref[f, z, t, r : r + rows, :]
    viscous = lambda z, t, r: pad_ref[3, z, t, r : r + rows, :]
    for t in range(3):
        for block in range(6):
            r = 8 + rows * block
            done = substep_block(cells, slot + 1, viscous, slot + 1, t, r, rows, flow, lane)
            for f in range(CHANNELS):
                half_ref[f, slot, t, r : r + rows, :] = done[f]


def second_pass(pad_ref, half_ref, slot, flow, store):
    rows = 32
    lane = lane_ids(rows)
    cells = lambda f, p, t, r: half_ref[f, p, t, r : r + rows, :]
    viscous = lambda p, t, r: pad_ref[3, p, t, r : r + rows, :]
    for t in range(2):
        for block in range(4):
            r = TOP + rows * block
            done = substep_block(cells, slot + 1, viscous, slot + 2, t, r, rows, flow, lane)
            for f in range(CHANNELS):
                store(f, slice(rows * block, rows * block + rows), slice(128 * t, 128 * t + 128), done[f])


def stencil_kernel(where_ref, flow_ref, *refs):
    block = Block(where_ref, *refs[:7])
    new_ref, pad_ref, half_ref = refs[7:]
    first, group = block.first, block.group

    def fill(z, carry):
        block.fill_own(pad_ref, z + 2, z)
        return carry

    lax.fori_loop(0, DEPTH, fill, 0)
    base = jnp.where(first, 10, 0)
    for j in range(2):
        block.fill_halo(pad_ref, base + j, j)
        block.fill_zero(pad_ref, 10 - base + j)

    def first_step(step, carry):
        at = step + jnp.where(first, 1, 0)
        first_pass(pad_ref, half_ref, at, 0.25 * flow_ref[group * DEPTH + at])
        return carry

    lax.fori_loop(0, 9, first_step, 0)
    block.fill_zero(half_ref, jnp.where(first, 0, 9))

    def second_step(z, carry):
        def store(f, rows, lanes, value):
            new_ref[f, z, rows, lanes] = value

        second_pass(pad_ref, half_ref, z, 0.25 * flow_ref[group * DEPTH + z + 1], store)
        return carry

    lax.fori_loop(0, DEPTH, second_step, 0)


def patchify(plane_ref, stage_ref):
    lane = lane_ids(8)
    for c in range(CHANNELS):
        for t in range(2):
            lines = [plane_ref[c, t, i:ROWS:PATCH, :] for i in range(PATCH)]
            for b in range(8):
                for u in range(2):
                    total = None
                    for i in range(8):
                        turn = 16 * ((i - b) % 8)
                        line = lines[8 * u + i]
                        line = pltpu.roll(line, turn, 1) if turn else line
                        total = line if total is None else jnp.where(lane // 16 == i, line, total)
                    stage_ref[2 * c + u, 8 * t + b : 128 : 16, :] = total


def sample_kernel(where_ref, flow_ref, *refs):
    block = Block(where_ref, *refs[:7])
    token_ref, pad_ref, half_ref, plane_ref, stage_ref = refs[7:]
    first, group = block.first, block.group

    def sample(s, carry):
        local = where_ref[1 + s] - group * DEPTH
        inside = (local >= 0) & (local < DEPTH)

        @pl.when(jnp.logical_not(inside))
        def _():
            token_ref[s] = jnp.zeros((128, PDIM), BF16)

        @pl.when(inside)
        def _():
            def fill(slot, c):
                z = local + slot - 2
                own = (z >= 0) & (z < DEPTH)
                halo = (first & (z >= DEPTH)) | (jnp.logical_not(first) & (z < 0))
                nothing = jnp.logical_not(own | halo)

                @pl.when(own)
                def _():
                    block.fill_own(pad_ref, slot, z)

                @pl.when(halo)
                def _():
                    block.fill_halo(pad_ref, slot, jnp.where(first, z - DEPTH, z + 2))

                @pl.when(nothing)
                def _():
                    block.fill_zero(pad_ref, slot)

                return c

            lax.fori_loop(0, 5, fill, 0)

            def first_step(slot, c):
                z = local + slot - 1
                outside = (first & (z < 0)) | (jnp.logical_not(first) & (z >= DEPTH))

                @pl.when(outside)
                def _():
                    block.fill_zero(half_ref, slot)

                @pl.when(jnp.logical_not(outside))
                def _():
                    first_pass(pad_ref, half_ref, slot, 0.25 * flow_ref[group * DEPTH + z + 1])

                return c

            lax.fori_loop(0, 3, first_step, 0)

            def store(f, rows, lanes, value):
                plane_ref[f, lanes.start // 128, rows, :] = value

            second_pass(pad_ref, half_ref, 0, 0.25 * flow_ref[group * DEPTH + local + 1], store)
            patchify(plane_ref, stage_ref)
            for u in range(6):
                token_ref[s, :, 128 * u : 128 * u + 128] = stage_ref[u].astype(BF16)

        return carry

    lax.fori_loop(0, 2, sample, 0)


def pack_columns_kernel(vel_ref, visc_ref, xlow_ref, xhigh_ref, low_ref, high_ref, low_stage, high_stage):
    low_stage[...] = jnp.zeros_like(low_stage)
    high_stage[...] = jnp.zeros_like(high_stage)

    def pack(rows, load, at):
        lane = lane_ids(rows)
        low = jnp.zeros((rows, 128), F32)
        high = low
        for f in range(4):
            for z in range(DEPTH):
                k = f * DEPTH + z
                pair = lane // 2
                low = jnp.where(pair == 32 + k, pltpu.roll(load(f, z, 1), (66 + 2 * k) % 128, 1), low)
                head = load(f, z, 0)
                high = jnp.where(pair == k, pltpu.roll(head, 2 * k, 1) if k else head, high)
        low_stage[at : at + rows, :] = low
        high_stage[at : at + rows, :] = high

    def inner(f, z, t):
        lanes = slice(128 * t, 128 * t + 128)
        return vel_ref[f, z, :, lanes] if f < CHANNELS else visc_ref[z, :, lanes]

    pack(ROWS, inner, TOP)
    pack(1, lambda f, z, t: xlow_ref[f, z, :, 128 * t : 128 * t + 128].astype(F32)[1:2], TOP - 1)
    pack(1, lambda f, z, t: xhigh_ref[f, z, :, 128 * t : 128 * t + 128].astype(F32)[0:1], TOP + ROWS)
    low_ref[...] = low_stage[...].astype(BF16)
    high_ref[...] = high_stage[...].astype(BF16)


def pack_edges_kernel(where_ref, low_ref, high_ref, xlow_ref, xhigh_ref, edge_ref, stage):
    edge_ref[:TALL] = low_ref[...] + high_ref[...]
    facing = jnp.where(where_ref[0] == 0, DEPTH - 1, 0)
    for f in range(4):
        for t in range(2):
            lanes = slice(128 * t, 128 * t + 128)
            at = 2 * f + t
            stage[at : at + 1] = xlow_ref[f, facing].astype(F32)[1:2, lanes]
            stage[8 + at : 9 + at] = xhigh_ref[f, facing].astype(F32)[0:1, lanes]
    edge_ref[TALL:] = stage[...].astype(BF16)


VMEM = pl.BlockSpec(memory_space=pltpu.VMEM)
SMEM = pl.BlockSpec(memory_space=pltpu.SMEM)


def local_call(kernel, name, out_shape, in_specs, scratch, us):
    return pl.pallas_call(
        kernel,
        out_shape=out_shape,
        in_specs=in_specs,
        out_specs=jax.tree.map(lambda _: VMEM, out_shape),
        scratch_shapes=scratch,
        compiler_params=pltpu.CompilerParams(vmem_limit_bytes=48 * 1024 * 1024),
        cost_estimate=pl.CostEstimate(flops=0, bytes_accessed=us * 3_000_000, transcendentals=0),
        name=name,
    )


def stencil(*operands):
    scratch = [pltpu.VMEM((4, 12, 3, TALL, 128), F32), pltpu.VMEM((CHANNELS, 10, 3, TALL, 128), F32)]
    shape = jax.ShapeDtypeStruct((CHANNELS, DEPTH, ROWS, COLS), F32)
    return local_call(stencil_kernel, "stencil", shape, [SMEM, SMEM] + [VMEM] * 7, scratch, 18)(*operands)


def sample_tokens(*operands):
    scratch = [
        pltpu.VMEM((4, 5, 3, TALL, 128), F32),
        pltpu.VMEM((CHANNELS, 3, 3, TALL, 128), F32),
        pltpu.VMEM((CHANNELS, 2, ROWS, 128), F32),
        pltpu.VMEM((6, 128, 128), F32),
    ]
    shape = jax.ShapeDtypeStruct((2, 128, PDIM), BF16)
    return local_call(sample_kernel, "sample", shape, [SMEM, SMEM] + [VMEM] * 7, scratch, 8)(*operands)


def pack_columns(*operands):
    shape = (jax.ShapeDtypeStruct((TALL, 128), BF16),) * 2
    scratch = [pltpu.VMEM((TALL, 128), F32)] * 2
    return local_call(pack_columns_kernel, "pack_columns", shape, [VMEM] * 4, scratch, 2)(*operands)


def pack_edges(*operands):
    shape = jax.ShapeDtypeStruct((TALL + 16, 128), BF16)
    scratch = [pltpu.VMEM((16, 128), F32)]
    return local_call(pack_edges_kernel, "pack_edges", shape, [SMEM] + [VMEM] * 4, scratch, 1)(*operands)


def layer_kernel(along_rows, n_tokens, n_cots, *refs):
    n = n_tokens + n_cots
    embed_ref, gain_ref, weight_ref, back_ref, out_ref = refs[n : n + 5]
    tokens, cots, normed, qk, vg = refs[n + 5 :]
    for whole, pieces in ((tokens, refs[:n_tokens]), (cots, refs[n_tokens:n])):
        at = 0
        for piece in pieces:
            whole[at : at + piece.shape[0], :] = piece[...]
            at += piece.shape[0]

    def project(c, carry):
        at = pl.multiple_of(c * 128, 128)
        embedded = jnp.dot(tokens[pl.ds(at, 128), :], embed_ref[...], preferred_element_type=F32).astype(BF16).astype(F32)
        centred = embedded - jnp.mean(embedded, axis=-1, keepdims=True)
        unit = centred * lax.rsqrt(jnp.mean(centred * centred, axis=-1, keepdims=True) + NORM_EPS)
        rows = (unit * gain_ref[...]).astype(BF16)
        normed[pl.ds(at, 128), :] = rows
        projected = jnp.dot(rows, weight_ref[...], preferred_element_type=F32).astype(BF16).astype(F32)
        back = lax.dot_general(
            cots[pl.ds(at, 128), :], back_ref[...], (((1,), (1,)), ((), ())), preferred_element_type=F32
        ).astype(BF16).astype(F32)
        qk[pl.ds(at, 128), :] = projected[:, :128]
        vg[pl.ds(at, 128), :] = projected[:, 128:] + back
        return carry

    lax.fori_loop(0, 8, project, 0)
    lane = lane_ids(128)
    low = lane < 64
    rowline = lax.broadcasted_iota(jnp.int32, (128, 128), 0) // 64
    same = rowline == lane // 64
    for p in range(8):
        if along_rows:
            load = lambda ref: jnp.concatenate([ref[2 * p : 1024 : 16, :], ref[2 * p + 1 : 1024 : 16, :]], axis=0)
        else:
            load = lambda ref: jnp.concatenate(
                [ref[128 * c + 16 * p : 128 * c + 16 * p + 16, :] for c in range(8)], axis=0
            )
        qk_wide, vg_wide = load(qk), load(vg)
        kq_wide, gv_wide = pltpu.roll(qk_wide, 64, 1), pltpu.roll(vg_wide, 64, 1)
        only_low = lambda a: jnp.where(low, a, 0.0).astype(BF16)
        only_high = lambda a: jnp.where(low, 0.0, a).astype(BF16)
        nt = (((1,), (1,)), ((), ()))
        tn = (((0,), (0,)), ((), ()))
        scores = lax.dot_general(only_low(qk_wide), kq_wide.astype(BF16), nt, preferred_element_type=F32)
        scores = scores * HEAD_DIM**-0.5
        if along_rows:
            scores = jnp.where(same, scores, -1e30)
        raised = jnp.exp(scores - jnp.max(scores, axis=-1, keepdims=True))
        probs = raised / jnp.sum(raised, axis=-1, keepdims=True)
        weights = probs.astype(BF16)
        dprob = lax.dot_general(only_low(gv_wide), vg_wide.astype(BF16), nt, preferred_element_type=F32)
        delta = jnp.sum(probs * dprob, axis=-1, keepdims=True)
        dscore = (probs * (dprob - delta) * HEAD_DIM**-0.5).astype(BF16)
        dqk = jnp.dot(dscore, only_low(kq_wide), preferred_element_type=F32) + lax.dot_general(
            dscore, only_high(kq_wide), tn, preferred_element_type=F32
        )
        dva = lax.dot_general(weights, only_low(gv_wide), tn, preferred_element_type=F32) + jnp.dot(
            weights, only_high(gv_wide), preferred_element_type=F32
        )
        for ref, value in ((qk, dqk), (vg, dva)):
            if along_rows:
                ref[2 * p : 1024 : 16, :] = value[:64]
                ref[2 * p + 1 : 1024 : 16, :] = value[64:]
            else:
                for c in range(8):
                    ref[128 * c + 16 * p : 128 * c + 16 * p + 16, :] = value[16 * c : 16 * c + 16]
    dqk, dva = qk[...].astype(BF16), vg[...].astype(BF16)
    tn = (((0,), (0,)), ((), ()))
    grad_output = lax.dot_general(dva, cots[...], tn, preferred_element_type=F32)[64:]
    low64 = lane_ids(64) < 64
    out_ref[:, :128] = lax.dot_general(normed[...], dqk, tn, preferred_element_type=F32).astype(BF16)
    values = lax.dot_general(normed[...], dva, tn, preferred_element_type=F32)
    for c in range(16):
        piece = grad_output[:, 128 * (c // 2) : 128 * (c // 2) + 128]
        if c % 2 == 0:
            piece = pltpu.roll(piece, 64, 1)
        out_ref[64 * c : 64 * c + 64, 128:] = jnp.where(low64, values[64 * c : 64 * c + 64], piece).astype(BF16)


def layer(along_rows, tokens, cots, *weights):
    kernel = functools.partial(layer_kernel, along_rows, len(tokens), len(cots))
    scratch = [
        pltpu.VMEM((1024, PDIM), BF16),
        pltpu.VMEM((1024, D), BF16),
        pltpu.VMEM((1024, D), BF16),
        pltpu.VMEM((1024, 128), F32),
        pltpu.VMEM((1024, 128), F32),
    ]
    name = "layer_rows" if along_rows else "layer_columns"
    operands = [*tokens, *cots, *weights]
    shape = jax.ShapeDtypeStruct((D, 256), BF16)
    return local_call(kernel, name, shape, [VMEM] * len(operands), scratch, 13)(*operands)


def around(k):
    return [(i, (i // 4) * 4 + (i + k) % 4) for i in range(8)]


ACROSS = [(i, i ^ 4) for i in range(8)]
PARTNER = [(i, i ^ 1) for i in range(8)]


def gather_pairs(mine, along_rows):
    axis = "tx" if along_rows else "ty"
    other = lax.ppermute(mine, axis, ACROSS if along_rows else PARTNER)
    pair = jnp.concatenate([mine, other], axis=0)
    moves = [around(k) if along_rows else shift(8, 2 * k) for k in (1, 2, 3)]
    return [pair] + [lax.ppermute(pair, axis, move) for move in moves]


def gather_rows(mine):
    other = lax.ppermute(mine, "tx", ACROSS)
    return [mine, other] + [lax.ppermute(a, "tx", around(k)) for k in (1, 2, 3) for a in (mine, other)]


def gather_columns(mine):
    chunks = [mine] + [lax.ppermute(mine, "ty", shift(8, k)) for k in (2, 4, 6)]
    return [b for a in chunks for b in (a, lax.ppermute(a, "ty", PARTNER))]


def head_weights(project_weight, output_weight, head):
    parts = [lax.dynamic_slice_in_dim(project_weight, part * D + head * HEAD_DIM, HEAD_DIM, 1) for part in range(3)]
    weight = jnp.concatenate(parts + [jnp.zeros((D, HEAD_DIM), BF16)], axis=1)
    back = lax.dynamic_slice_in_dim(output_weight, head * HEAD_DIM, HEAD_DIM, 0)
    return weight, jnp.concatenate([jnp.zeros((HEAD_DIM, D), BF16), back], axis=0)


def shards(
    velocity, viscosity, mean_flow, plane_pick, embed_weight, norm_gain, project_weight, output_weight, cotangent
):
    group, row, column = lax.axis_index("grp"), lax.axis_index("tx"), lax.axis_index("ty")

    def planes(begin, count):
        cut = [
            lax.dynamic_slice_in_dim(velocity, begin, count, 1),
            lax.dynamic_slice_in_dim(viscosity, begin, count, 0)[None],
        ]
        return jnp.concatenate(cut, axis=0).astype(BF16)

    def cells(rows, columns):
        cut = [velocity[:, :, rows, columns], viscosity[None, :, rows, columns]]
        return jnp.concatenate(cut, axis=0).astype(BF16)

    every = slice(None)
    zhalo = lax.ppermute(planes((1 - group) * (DEPTH - 2), 2), "grp", SWAP)
    xlow = lax.ppermute(cells(slice(ROWS - 2, ROWS), every), "tx", shift(8, 1))
    xhigh = lax.ppermute(cells(slice(0, 2), every), "tx", shift(8, -1))
    low, high = pack_columns(velocity, viscosity, xlow, xhigh)
    low = lax.ppermute(low, "ty", shift(8, 1))
    high = lax.ppermute(high, "ty", shift(8, -1))
    where = jnp.concatenate([group[None].astype(jnp.int32), plane_pick])
    flow = jnp.pad(mean_flow, 1)
    edges = pack_edges(where, low, high, xlow, xhigh)
    zedge = lax.ppermute(edges, "grp", SWAP)
    halos = (zhalo, xlow, xhigh, edges[:TALL], zedge)
    sampled = sample_tokens(where, flow, velocity, viscosity, *halos)
    kept = lax.dynamic_index_in_dim(sampled, group, 0, keepdims=False)
    sent = lax.dynamic_index_in_dim(sampled, 1 - group, 0, keepdims=False)
    tokens = kept + lax.ppermute(sent, "grp", SWAP)
    cots = cotangent.reshape(128, D)
    gain = norm_gain[None]
    outs = []
    for along_rows, head in ((True, row), (False, 8 + column)):
        gather = gather_rows if along_rows else gather_columns
        weight, back = head_weights(project_weight, output_weight, head)
        outs.append(
            layer(along_rows, gather(tokens), gather_pairs(cots, along_rows), embed_weight, gain, weight, back)
        )
    partial = jnp.concatenate(outs, axis=1).reshape(128, 8, 512)
    partial, late = lax.optimization_barrier((partial, where))
    new_velocity = stencil(late, flow, velocity, viscosity, *halos)
    arrived = lax.all_to_all(partial, ("grp", "tx", "ty"), split_axis=0, concat_axis=0, tiled=True)
    arrived = arrived.reshape(2, 8, 8, 8, 512).astype(F32)
    heads = jnp.concatenate(
        [jnp.sum(arrived[..., :256], axis=(0, 2)), jnp.sum(arrived[..., 256:], axis=(0, 1))], axis=0
    )
    grad_project = heads[..., :192].reshape(HEADS, 8, 3, HEAD_DIM).transpose(1, 2, 0, 3).reshape(8, 3 * D)
    pieces = lax.all_to_all(heads[..., 192:], ("grp", "tx"), split_axis=0, concat_axis=0, tiled=True)
    grad_output = pieces.transpose(1, 0, 2).reshape(8, D)
    first_row = ((group * 8 + row) * 8 + column) * 8
    weight_rows = lax.dynamic_slice_in_dim(project_weight, first_row, 8, 0).astype(F32)
    gains = lax.dynamic_slice_in_dim(norm_gain, first_row, 8, 0)
    grad_gain = jnp.sum(weight_rows * grad_project, axis=1) / gains
    return new_velocity, grad_project, grad_output, grad_gain


def solution(mesh):
    in_specs = (
        P(None, "grp", "tx", "ty"),
        P("grp", "tx", "ty"),
        P(),
        P(),
        P(),
        P(),
        P(),
        P(),
        P("grp", "tx", "ty", None),
    )
    out_specs = (
        P(None, "grp", "tx", "ty"),
        P(("grp", "tx", "ty"), None),
        P(("grp", "tx", "ty"), None),
        P(("grp", "tx", "ty")),
    )
    return jax.shard_map(shards, mesh=mesh, in_specs=in_specs, out_specs=out_specs, check_vma=False)
```

```python
import functools

import jax
import jax.numpy as jnp
from jax import lax
from jax.experimental import pallas as pl
from jax.experimental.pallas import tpu as pltpu
from jax.sharding import PartitionSpec as P


D = 1024
CHANNELS = 3
HEAD_DIM = 64
PDIM = 768
DEPTH = 8
ROWS = 128
COLS = 256
NORM_EPS = 1e-06
F32 = jnp.float32
BF16 = jnp.bfloat16


TOP = 16
TALL = 160


def shift(count, step):
    return [(i, (i + step) % count) for i in range(count)]


SWAP = [(0, 1), (1, 0)]


VMEM = pl.BlockSpec(memory_space=pltpu.VMEM)
SMEM = pl.BlockSpec(memory_space=pltpu.SMEM)
ANY = pl.BlockSpec(memory_space=pl.ANY)
HBM = pl.BlockSpec(memory_space=pltpu.HBM)


NN = (((1,), (0,)), ((), ()))
NT = (((1,), (1,)), ((), ()))
TN = (((0,), (0,)), ((), ()))


def dot(a, b, dims=NN):
    return lax.dot_general(a, b, dims, preferred_element_type=F32)


def lane_ids(rows):
    return lax.broadcasted_iota(jnp.int32, (rows, 128), 1)


def beside(tiles, wanted, lane):
    forward = [pltpu.roll(tile, 127, 1) for tile in tiles]
    backward = [pltpu.roll(tile, 1, 1) for tile in tiles]
    following = [jnp.where(lane == 127, forward[(t + 1) % 3], forward[t]) for t in wanted]
    preceding = [jnp.where(lane == 0, backward[(t + 2) % 3], backward[t]) for t in wanted]
    return following, preceding


def substep_block(cells, plane, viscous, vplane, row, flow, lane, wanted):
    here = [viscous(vplane, t, row) for t in range(3)]
    following, preceding = beside(here, wanted, lane)
    faces, keep = [], []
    for t in wanted:
        sides = (
            viscous(vplane + 1, t, row),
            viscous(vplane - 1, t, row),
            viscous(vplane, t, row + 1),
            viscous(vplane, t, row - 1),
            following[t],
            preceding[t],
        )
        face = [here[t] + side for side in sides]
        keep.append(1.0 - (((face[0] + face[1]) + (face[2] + face[3])) + (face[4] + face[5])))
        face[2] = face[2] - flow
        face[3] = face[3] + flow
        faces.append(face)
    results = []
    for f in range(CHANNELS):
        centre = [cells(f, plane, t, row) for t in range(3)]
        following, preceding = beside(centre, wanted, lane)
        for t in wanted:
            face = faces[t]
            total = keep[t] * centre[t] + face[0] * cells(f, plane + 1, t, row)
            total = total + face[1] * cells(f, plane - 1, t, row)
            total = total + face[2] * cells(f, plane, t, row + 1)
            total = total + face[3] * cells(f, plane, t, row - 1)
            total = total + face[4] * following[t]
            total = total + face[5] * preceding[t]
            results.append((f, t, total))
    return results


def edge_tile(packed, k, lane):
    turned = pltpu.roll(packed, lax.rem(126 - 4 * k + 128, 128), 1)
    return jnp.where((lane < 2) | (lane >= 126), turned, 0.0)


class Block:
    def __init__(self, where_ref, zhalo_ref, xlow_ref, xhigh_ref, packed_ref, zedge_ref):
        self.group = where_ref[0]
        self.first = self.group == 0
        self.zhalo, self.xlow, self.xhigh, self.packed, self.zedge = zhalo_ref, xlow_ref, xhigh_ref, packed_ref, zedge_ref

    def fill_own(self, pad_ref, slot, z, load):
        packed = self.packed[...].astype(F32)
        lane = lane_ids(TALL)
        for f in range(4):
            scale = 1.0 if f < CHANNELS else 0.25
            source = load(f) * scale if f == CHANNELS else load(f)
            low = self.xlow[f, z].astype(F32) * scale
            high = self.xhigh[f, z].astype(F32) * scale
            for t in range(2):
                lanes = slice(128 * t, 128 * t + 128)
                pad_ref[f, slot, t, TOP : TOP + ROWS, :] = source[:, lanes]
                pad_ref[f, slot, t, TOP - 2 : TOP, :] = low[:, lanes]
                pad_ref[f, slot, t, TOP + ROWS : TOP + ROWS + 2, :] = high[:, lanes]
            pad_ref[f, slot, 2] = edge_tile(packed, f * DEPTH + z, lane) * scale

    def fill_halo(self, pad_ref, slot, j):
        packed = self.zedge[:TALL].astype(F32)
        edges = self.zedge[TALL:].astype(F32)
        lane = lane_ids(TALL)
        facing = jnp.where(self.first, 0, DEPTH - 1)
        for f in range(4):
            scale = 1.0 if f < CHANNELS else 0.25
            for t in range(2):
                lanes = slice(128 * t, 128 * t + 128)
                at = 2 * f + t
                pad_ref[f, slot, t, TOP : TOP + ROWS, :] = self.zhalo[f, j, :, lanes].astype(F32) * scale
                pad_ref[f, slot, t, TOP - 1 : TOP, :] = edges[at : at + 1] * scale
                pad_ref[f, slot, t, TOP + ROWS : TOP + ROWS + 1, :] = edges[8 + at : 9 + at] * scale
            pad_ref[f, slot, 2] = edge_tile(packed, f * DEPTH + facing, lane) * scale

    def fill_zero(self, pad_ref, slot):
        for f in range(pad_ref.shape[0]):
            for t in range(3):
                pad_ref[f, slot, t] = jnp.zeros((TALL, 128), F32)


def first_pass(pad_ref, half_ref, slot, flow, rim=True):
    lane = lane_ids(8)
    cells = lambda f, z, t, r: pad_ref[f, z, t, r : r + 8, :]
    viscous = lambda z, t, r: pad_ref[3, z, t, r : r + 8, :]
    rows = range(TOP - 8, TOP + ROWS + 8, 8) if rim else range(TOP, TOP + ROWS, 8)
    for row in rows:
        for f, t, done in substep_block(cells, slot + 1, viscous, slot + 1, row, flow, lane, (0, 1, 2) if rim else (0, 1)):
            half_ref[f, slot, t, row : row + 8, :] = done


def second_pass(pad_ref, half_ref, slot, flow, store):
    lane = lane_ids(8)
    cells = lambda f, p, t, r: half_ref[f, p, t, r : r + 8, :]
    viscous = lambda p, t, r: pad_ref[3, p, t, r : r + 8, :]
    for row in range(0, ROWS, 8):
        for f, t, done in substep_block(cells, slot + 1, viscous, slot + 2, TOP + row, flow, lane, (0, 1)):
            store(f, slice(row, row + 8), slice(128 * t, 128 * t + 128), done)


def stencil_kernel(where_ref, flow_ref, vel_ref, visc_ref, *refs):
    block = Block(where_ref, *refs[:5])
    new_ref, pad_ref, half_ref = refs[5:]
    first, group = block.first, block.group

    def fill(z, carry):
        block.fill_own(pad_ref, z + 2, z, lambda f: vel_ref[f, z] if f < CHANNELS else visc_ref[z])
        return carry

    lax.fori_loop(0, DEPTH, fill, 0)
    base = jnp.where(first, 10, 0)
    for j in range(2):
        block.fill_halo(pad_ref, base + j, j)
        block.fill_zero(pad_ref, 10 - base + j)

    def first_step(step, carry):
        at = step + jnp.where(first, 1, 0)
        first_pass(pad_ref, half_ref, at, 0.25 * flow_ref[group * DEPTH + at])
        return carry

    lax.fori_loop(0, 9, first_step, 0)
    block.fill_zero(half_ref, jnp.where(first, 0, 9))

    def second_step(z, carry):
        def store(f, rows, lanes, value):
            new_ref[f, z, rows, lanes] = value

        second_pass(pad_ref, half_ref, z, 0.25 * flow_ref[group * DEPTH + z + 1], store)
        return carry

    lax.fori_loop(0, DEPTH, second_step, 0)


def reorder(count, inner):
    row = lax.broadcasted_iota(jnp.int32, (count, count), 0)
    column = lax.broadcasted_iota(jnp.int32, (count, count), 1)
    outer = count // inner
    return (column == row % outer * inner + row // outer).astype(BF16)


def patchify(plane_ref, stage_ref, write):
    piece = lane_ids(8) // 16
    spread = reorder(128, 16)
    for c in range(CHANNELS):
        for t in range(2):
            turned = dot(spread, plane_ref[c, t].astype(BF16))
            for u in range(2):
                lines = [turned[64 * u + 8 * i : 64 * u + 8 * i + 8] for i in range(8)]
                for s in (1, 2, 4):
                    lower = (piece // s) % 2 == 0
                    for i in range(8):
                        if i & s == 0:
                            a, b = lines[i], lines[i + s]
                            lines[i] = jnp.where(lower, a, pltpu.roll(b, 16 * s, 1))
                            lines[i + s] = jnp.where(lower, pltpu.roll(a, 128 - 16 * s, 1), b)
                for b in range(8):
                    stage_ref[2 * c + u, 64 * t + 8 * b : 64 * t + 8 * b + 8, :] = lines[b]
    gather = reorder(128, 8)
    for u in range(6):
        write(u, dot(gather, stage_ref[u].astype(BF16)).astype(BF16))


def sample_kernel(where_ref, flow_ref, vel_ref, visc_ref, *refs):
    block = Block(where_ref, *refs[:5])
    kept_ref, sent_ref, pad_ref, half_ref, plane_ref, stage_ref, token_ref = refs[5:]
    first, group = block.first, block.group

    def sample(s, carry):
        local = where_ref[1 + s] - group * DEPTH
        inside = (local >= 0) & (local < DEPTH)

        def write(value):
            @pl.when(s == group)
            def _():
                value(kept_ref)

            @pl.when(s != group)
            def _():
                value(sent_ref)

        def write_zeros(ref):
            ref[...] = jnp.zeros((128, PDIM), BF16)

        def write_patches(ref):
            for u in range(6):
                ref[:, 128 * u : 128 * u + 128] = token_ref[u]

        @pl.when(jnp.logical_not(inside))
        def _():
            write(write_zeros)

        @pl.when(inside)
        def _():
            def fill(slot, c):
                z = local + slot - 2
                own = (z >= 0) & (z < DEPTH)
                halo = (first & (z >= DEPTH)) | (jnp.logical_not(first) & (z < 0))
                nothing = jnp.logical_not(own | halo)

                @pl.when(own)
                def _():
                    block.fill_own(pad_ref, slot, z, lambda f: vel_ref[f, z] if f < CHANNELS else visc_ref[z])

                @pl.when(halo)
                def _():
                    block.fill_halo(pad_ref, slot, jnp.where(first, z - DEPTH, z + 2))

                @pl.when(nothing)
                def _():
                    block.fill_zero(pad_ref, slot)

                return c

            lax.fori_loop(0, 5, fill, 0)

            def first_step(step, c):
                slot = 2 * step
                z = local + slot - 1
                outside = (first & (z < 0)) | (jnp.logical_not(first) & (z >= DEPTH))

                @pl.when(outside)
                def _():
                    block.fill_zero(half_ref, slot)

                @pl.when(jnp.logical_not(outside))
                def _():
                    first_pass(pad_ref, half_ref, slot, 0.25 * flow_ref[group * DEPTH + z + 1], rim=False)

                return c

            lax.fori_loop(0, 2, first_step, 0)
            first_pass(pad_ref, half_ref, 1, 0.25 * flow_ref[group * DEPTH + local + 1])

            def store(f, rows, lanes, value):
                plane_ref[f, lanes.start // 128, rows, :] = value

            second_pass(pad_ref, half_ref, 0, 0.25 * flow_ref[group * DEPTH + local + 1], store)

            def hold(u, value):
                token_ref[u] = value

            patchify(plane_ref, stage_ref, hold)
            write(write_patches)

        return carry

    lax.fori_loop(0, 2, sample, 0)


def pack_planes_kernel(vel_ref, visc_ref, plane_ref, stage, sems):
    begin = (1 - lax.axis_index("grp")) * (DEPTH - 2)
    copies = (
        pltpu.make_async_copy(vel_ref.at[:, pl.ds(begin, 2)], stage.at[:CHANNELS], sems.at[0]),
        pltpu.make_async_copy(visc_ref.at[pl.ds(begin, 2)], stage.at[CHANNELS], sems.at[1]),
    )
    for copy in copies:
        copy.start()
    for copy in copies:
        copy.wait()
    plane_ref[...] = stage[...].astype(BF16)


def pack_planes(velocity, viscosity):
    shape = jax.ShapeDtypeStruct((4, 2, ROWS, COLS), BF16)
    scratch = [pltpu.VMEM((4, 2, ROWS, COLS), F32), pltpu.SemaphoreType.DMA((2,))]
    return local_call(pack_planes_kernel, shape, [ANY] * 2, scratch, 2, 60)(velocity, viscosity)


def pack_rows_kernel(vel_head, vel_tail, visc_hbm, head_ref, tail_ref, visc_ref, sems):
    copies = [
        pltpu.make_async_copy(visc_hbm.at[:, pl.ds(at, 8)], visc_ref.at[i], sems.at[i])
        for i, at in enumerate((0, ROWS - 8))
    ]
    for copy in copies:
        copy.start()
    for f in range(CHANNELS):
        head_ref[f] = vel_head[f, :, :2].astype(BF16)
        tail_ref[f] = vel_tail[f, :, 6:].astype(BF16)
    for copy in copies:
        copy.wait()
    head_ref[CHANNELS] = visc_ref[0, :, :2].astype(BF16)
    tail_ref[CHANNELS] = visc_ref[1, :, 6:].astype(BF16)


def pack_rows(velocity, viscosity):
    block = lambda at: pl.BlockSpec((CHANNELS, DEPTH, 8, COLS), lambda i: (0, 0, at, 0))
    return pl.pallas_call(
        pack_rows_kernel,
        grid=(1,),
        out_shape=(jax.ShapeDtypeStruct((4, DEPTH, 2, COLS), BF16),) * 2,
        in_specs=[block(0), block(ROWS // 8 - 1), HBM],
        out_specs=(VMEM,) * 2,
        scratch_shapes=[pltpu.VMEM((2, DEPTH, 8, COLS), F32), pltpu.SemaphoreType.DMA((2,))],
        compiler_params=pltpu.CompilerParams(vmem_limit_bytes=24 * 1024 * 1024),
        cost_estimate=pl.CostEstimate(flops=0, bytes_accessed=3_000_000, transcendentals=0),
        name="pack_rows",
    )(velocity, velocity, viscosity)


def pack_columns_kernel(vel_ref, visc_hbm, xlow_ref, xhigh_ref, low_ref, high_ref, low_stage, high_stage, visc_ref, sem):
    copy = pltpu.make_async_copy(visc_hbm, visc_ref, sem)
    copy.start()
    low_stage[...] = jnp.zeros_like(low_stage)
    high_stage[...] = jnp.zeros_like(high_stage)

    def pack(rows, load, fields, low, high):
        lane = lane_ids(rows)
        for f in fields:
            for z in range(DEPTH):
                k = f * DEPTH + z
                pair = lane // 2
                low = jnp.where(pair == 2 * k, pltpu.roll(load(f, z, 1), (4 * k + 2) % 128, 1), low)
                high = jnp.where(pair == 2 * k + 1, pltpu.roll(load(f, z, 0), 4 * k + 2, 1), high)
        return low, high

    def inner(f, z, t):
        lanes = slice(128 * t, 128 * t + 128)
        return vel_ref[f, z, :, lanes] if f < CHANNELS else visc_ref[z, :, lanes]

    nothing = jnp.zeros((1, 128), F32)
    for at, halo_ref, row in ((TOP - 1, xlow_ref, 1), (TOP + ROWS, xhigh_ref, 0)):
        load = lambda f, z, t: halo_ref[f, z, :, 128 * t : 128 * t + 128].astype(F32)[row : row + 1]
        low_stage[at : at + 1], high_stage[at : at + 1] = pack(1, load, range(4), nothing, nothing)
    nothing = jnp.zeros((ROWS, 128), F32)
    low, high = pack(ROWS, inner, range(CHANNELS), nothing, nothing)
    copy.wait()
    rows = slice(TOP, TOP + ROWS)
    low_stage[rows], high_stage[rows] = pack(ROWS, inner, (CHANNELS,), low, high)
    low_ref[...] = low_stage[...].astype(BF16)
    high_ref[...] = high_stage[...].astype(BF16)


def pack_edges_kernel(where_ref, low_ref, high_ref, xlow_ref, xhigh_ref, edge_ref, stage):
    edge_ref[:TALL] = low_ref[...] + high_ref[...]
    facing = jnp.where(where_ref[0] == 0, DEPTH - 1, 0)
    for f in range(4):
        for t in range(2):
            lanes = slice(128 * t, 128 * t + 128)
            at = 2 * f + t
            stage[at : at + 1] = xlow_ref[f, facing].astype(F32)[1:2, lanes]
            stage[8 + at : 9 + at] = xhigh_ref[f, facing].astype(F32)[0:1, lanes]
    edge_ref[TALL:] = stage[...].astype(BF16)


def local_call(kernel, out_shape, in_specs, scratch, us, mib):
    return pl.pallas_call(
        kernel,
        out_shape=out_shape,
        in_specs=in_specs,
        out_specs=jax.tree.map(lambda _: VMEM, out_shape),
        scratch_shapes=scratch,
        compiler_params=pltpu.CompilerParams(vmem_limit_bytes=mib * 1024 * 1024),
        cost_estimate=pl.CostEstimate(flops=0, bytes_accessed=us * 3_000_000, transcendentals=0),
    )


def stencil(*operands):
    scratch = [pltpu.VMEM((4, 12, 3, TALL, 128), F32), pltpu.VMEM((CHANNELS, 10, 3, TALL, 128), F32)]
    shape = jax.ShapeDtypeStruct((CHANNELS, DEPTH, ROWS, COLS), F32)
    return local_call(stencil_kernel, shape, [SMEM, SMEM] + [VMEM] * 7, scratch, 12, 48)(*operands)


def sample_tokens(*operands):
    scratch = [
        pltpu.VMEM((4, 5, 3, TALL, 128), F32),
        pltpu.VMEM((CHANNELS, 3, 3, TALL, 128), F32),
        pltpu.VMEM((CHANNELS, 2, ROWS, 128), F32),
        pltpu.VMEM((6, 128, 128), F32),
        pltpu.VMEM((6, 128, 128), BF16),
    ]
    shape = (jax.ShapeDtypeStruct((128, PDIM), BF16),) * 2
    specs = [SMEM, SMEM] + [VMEM] * 7
    return local_call(sample_kernel, shape, specs, scratch, 7, 32)(*operands)


def pack_columns(*operands):
    shape = (jax.ShapeDtypeStruct((TALL, 128), BF16),) * 2
    scratch = [pltpu.VMEM((TALL, 128), F32)] * 2 + [pltpu.VMEM((DEPTH, ROWS, COLS), F32), pltpu.SemaphoreType.DMA]
    return local_call(pack_columns_kernel, shape, [VMEM, HBM, VMEM, VMEM], scratch, 2, 24)(*operands)


def pack_edges(*operands):
    shape = jax.ShapeDtypeStruct((TALL + 16, 128), BF16)
    scratch = [pltpu.VMEM((16, 128), F32)]
    return local_call(pack_edges_kernel, shape, [SMEM] + [VMEM] * 4, scratch, 1, 24)(*operands)


def rounded(a):
    return a.astype(BF16).astype(F32)


def layer_kernel(along_rows, n_tokens, n_cots, *refs):
    n = n_tokens + n_cots
    embed_hbm, project_hbm, output_hbm, gain_ref = refs[n : n + 4]
    other = refs[n + 4 : n + 6] if along_rows else ()
    outs = refs[n + 6 : n + 7] if along_rows else refs[n + 4 : n + 6]
    (
        tokens, cots, normed, qk, vg, weight, emb_even, emb_odd, rows_even, rows_odd, embed_ref, pair_ref, back_ref,
        sems,
    ) = refs[n + 4 + len(other) + len(outs) :]
    head = lax.axis_index("tx") if along_rows else 8 + lax.axis_index("ty")
    started = []

    def start(source, target):
        started.append(pltpu.make_async_copy(source, target, sems.at[len(started)]))
        started[-1].start()

    start(embed_hbm, embed_ref)
    at = 0
    for piece in refs[:n_tokens]:
        start(piece, tokens.at[pl.ds(at, piece.shape[0])])
        at += piece.shape[0]
    for part in range(3):
        columns = pl.ds(pl.multiple_of(part * D + (head // 2) * 128, 128), 128)
        start(project_hbm.at[:, columns], pair_ref.at[part])
    start(output_hbm.at[pl.ds(pl.multiple_of(head * HEAD_DIM, HEAD_DIM), HEAD_DIM)], back_ref)
    first_cot = len(started)
    at = 0
    for piece in refs[n_tokens:n]:
        start(piece, cots.at[pl.ds(at, piece.shape[0])])
        at += piece.shape[0]
    lane = lane_ids(128)
    low = lane < 64

    def choose(is_odd):
        def rows(c, carry):
            at = pl.ds(pl.multiple_of(c * 128, 128), 128)
            query, key, value = (pair_ref[part, at, :].astype(F32) for part in range(3))
            turn = lambda a: pltpu.roll(a, 64, 1)
            query, key, value = (turn(query), key, turn(value)) if is_odd else (query, turn(key), value)
            weight[at, :128] = jnp.where(low, query, key).astype(BF16)
            weight[at, 128:] = jnp.where(low, value, 0.0).astype(BF16)
            return carry

        lax.fori_loop(0, 8, rows, 0)

    def chunk(c):
        return pl.ds(pl.multiple_of(lax.rem(c, 4) * 256, 256), 256)

    def embed(c, emb):
        emb[...] = dot(tokens[chunk(c), :], embed_ref[...]).astype(BF16)

    def normalise(c, emb, rows_ref):
        embedded = emb[...].astype(F32)
        centred = embedded - jnp.mean(embedded, axis=-1, keepdims=True)
        unit = centred * lax.rsqrt(jnp.mean(centred * centred, axis=-1, keepdims=True) + NORM_EPS)
        rows = (unit * gain_ref[...]).astype(BF16)
        rows_ref[...] = rows
        normed[chunk(c), :] = rows

    sorted_rows = (lambda a: dot(reorder(256, 16), a.astype(BF16))) if along_rows else (lambda a: a)

    def project(c, rows_ref):
        keep = lane_ids(256) < 64
        projected = rounded(dot(rows_ref[...], weight[...]))
        back = rounded(dot(cots[chunk(c), :], back_ref[...], NT))
        values = jnp.where(keep, projected[:, 128:], jnp.concatenate([back, back], axis=1))
        if along_rows:
            both = sorted_rows(jnp.concatenate([projected[:, :128], values], axis=1))
            qk[chunk(c), :] = both[:, :128]
            vg[chunk(c), :] = both[:, 128:]
        else:
            qk[chunk(c), :] = projected[:, :128]
            vg[chunk(c), :] = values

    def landed(pieces, count, whole, base, c):
        rows = 1024 // count
        for k in range(count // 4):
            piece = count // 4 * c + k
            target = whole.at[pl.ds(pl.multiple_of(piece * rows, rows), rows)]
            pltpu.make_async_copy(pieces[0], target, sems.at[base + piece]).wait()

    token_landed = lambda c: landed(refs[:n_tokens], n_tokens, tokens, 1, c)
    cot_landed = lambda c: landed(refs[n_tokens:n], n_cots, cots, first_cot, c)
    started[0].wait()
    token_landed(0)
    embed(0, emb_even)
    for copy in started[n_tokens + 1 : first_cot]:
        copy.wait()
    odd = lax.rem(head, 2) == 1

    @pl.when(odd)
    def _():
        choose(True)

    @pl.when(jnp.logical_not(odd))
    def _():
        choose(False)

    def step(i, carry):
        c = 2 * i
        token_landed(c + 1)

        @pl.when(i == 0)
        def _():
            token_landed(2)

        cot_landed(c)
        cot_landed(c + 1)
        embed(c + 1, emb_odd)
        normalise(c, emb_even, rows_even)
        project(jnp.maximum(c - 1, 0), rows_odd)
        embed(c + 2, emb_even)
        normalise(c + 1, emb_odd, rows_odd)
        project(c, rows_even)
        return carry

    lax.fori_loop(0, 2, step, 0)
    project(3, rows_odd)
    if along_rows:
        row = lax.broadcasted_iota(jnp.int32, (128, 128), 0)
        same = (row // 16) % 2 == (lane // 16) % 2
        spots = lambda p: [256 * c + 32 * p for c in range(4)]
        size = 32
    else:
        spots = lambda p: [128 * c + 16 * p for c in range(8)]
        size = 16
    only_low = lambda a: jnp.where(low, a, 0.0).astype(BF16)
    only_high = lambda a: jnp.where(low, 0.0, a).astype(BF16)

    def load(ref, p):
        return jnp.concatenate([ref[at : at + size, :] for at in spots(p)], axis=0)

    def store(ref, p, value):
        for k, at in enumerate(spots(p)):
            ref[at : at + size, :] = value[size * k : size * k + size]

    for first in range(0, 8, 4):
        blocks = range(first, first + 4)
        wide = [(load(qk, p), load(vg, p)) for p in blocks]
        turned = [(pltpu.roll(a, 64, 1), pltpu.roll(b, 64, 1)) for a, b in wide]
        scores = [dot(only_low(a), t.astype(BF16), NT) * HEAD_DIM**-0.5 for (a, _), (t, _) in zip(wide, turned)]
        dprobs = [dot(only_low(t), b.astype(BF16), NT) for (_, b), (_, t) in zip(wide, turned)]
        if along_rows:
            scores = [jnp.where(same, a, -1e30) for a in scores]
        raised = [jnp.exp(a - jnp.max(a, axis=-1, keepdims=True)) for a in scores]
        probs = [a / jnp.sum(a, axis=-1, keepdims=True) for a in raised]
        deltas = [jnp.sum(a * d, axis=-1, keepdims=True) for a, d in zip(probs, dprobs)]
        weights = [a.astype(BF16) for a in probs]
        dscores = [(a * (d - e) * HEAD_DIM**-0.5).astype(BF16) for a, d, e in zip(probs, dprobs, deltas)]
        dqk = [dot(d, only_low(t)) + dot(d, only_high(t), TN) for d, (t, _) in zip(dscores, turned)]
        dva = [dot(w, only_low(t), TN) + dot(w, only_high(t)) for w, (_, t) in zip(weights, turned)]
        for p, a, b in zip(blocks, dqk, dva):
            store(qk, p, a)
            store(vg, p, b)
    both = jnp.concatenate([qk[...].astype(BF16), vg[...].astype(BF16)], axis=1)
    if along_rows:
        unsort = reorder(256, 16)
        both = jnp.concatenate([dot(unsort, both[256 * c : 256 * c + 256]).astype(BF16) for c in range(4)], axis=0)
    grad_output = dot(both[:, 128:], cots[...], TN)[64:]
    grad_project = dot(normed[...], both, TN)
    if not along_rows:
        outs[0][...] = grad_project.astype(BF16)
        outs[1][...] = grad_output
        return
    low64 = lane_ids(64) < 64
    out_ref, (other_project, other_output) = outs[0], other
    out_ref[:, :128] = grad_project[:, :128].astype(BF16)
    out_ref[:, 256:384] = other_project[:, :128]
    for c in range(16):
        rows = slice(64 * c, 64 * c + 64)
        lanes = slice(128 * (c % 8), 128 * (c % 8) + 128)
        piece = grad_output[:, lanes] if c < 8 else other_output[:, lanes]
        out_ref[rows, 128:256] = jnp.where(low64, grad_project[rows, 128:], pltpu.roll(piece, 64, 1)).astype(BF16)
        out_ref[rows, 384:] = jnp.where(low64, other_project[rows, 128:].astype(F32), piece).astype(BF16)


def layer(tokens, cots, embed_weight, project_weight, output_weight, gain, other=None):
    along_rows = other is not None
    kernel = functools.partial(layer_kernel, along_rows, len(tokens), len(cots))
    shapes = (((D, 512), BF16),) if along_rows else (((D, 256), BF16), ((HEAD_DIM, D), F32))
    operands = [*tokens, *cots, embed_weight, project_weight, output_weight]
    others = (gain,) + (other or ())
    chunk = [pltpu.VMEM((256, D), BF16)] * 4
    scratch = [
        pltpu.VMEM((1024, PDIM), BF16),
        pltpu.VMEM((1024, D), BF16),
        pltpu.VMEM((1024, D), BF16),
        pltpu.VMEM((1024, 128), F32),
        pltpu.VMEM((1024, 128), F32),
        pltpu.VMEM((D, 256), BF16),
        *chunk,
        pltpu.VMEM((PDIM, D), BF16),
        pltpu.VMEM((3, D, 128), BF16),
        pltpu.VMEM((HEAD_DIM, D), BF16),
        pltpu.SemaphoreType.DMA((len(operands) + 2,)),
    ]
    return local_call(
        kernel,
        tuple(jax.ShapeDtypeStruct(*shape) for shape in shapes),
        [ANY] * len(operands) + [VMEM] * len(others),
        scratch,
        11,
        60,
    )(*operands, *others)


def finish_kernel(arrived_ref, weight_ref, gain_ref, project_ref, piece_ref, norm_ref):
    low = lane_ids(8) < 64
    part = lambda g, x, y, tile: arrived_ref[64 * g + 8 * x + y, :, 128 * tile : 128 * tile + 128].astype(F32)

    def total(head, tile, along_rows):
        spots = [(g, head, m) if along_rows else (g, m, head) for g in range(2) for m in range(8)]
        values = [part(*spot, tile) for spot in spots]
        while len(values) > 1:
            values = [a + b for a, b in zip(values[::2], values[1::2])]
        return values[0]

    turn = lambda a: pltpu.roll(a, 64, 1)
    first = lax.axis_index("grp") == 0
    gain_total = jnp.zeros((8, 1), F32)
    for along_rows in (True, False):
        tile = 0 if along_rows else 2
        for m in range(4):
            pair = []
            for h in (2 * m, 2 * m + 1):
                pair.append((total(h, tile, along_rows), total(h, tile + 1, along_rows)))
                spare = total(h, 3 - tile, along_rows)
                one, two = (pair[-1][1], spare) if along_rows else (spare, pair[-1][1])

                @pl.when(first if along_rows else jnp.logical_not(first))
                def _():
                    piece_ref[h] = jnp.where(low, turn(one), two)

            (qk_even, v_even), (qk_odd, v_odd) = pair
            columns = (
                jnp.where(low, qk_even, turn(qk_odd)),
                jnp.where(low, turn(qk_even), qk_odd),
                jnp.where(low, v_even, turn(v_odd)),
            )
            for k, value in enumerate(columns):
                at = D * k + 128 * m + (0 if along_rows else 512)
                project_ref[:, at : at + 128] = value
                weight = weight_ref[:, at : at + 128].astype(F32)
                gain_total = gain_total + jnp.sum(weight * value, axis=1, keepdims=True)
    norm_ref[...] = gain_total / gain_ref[...]


def finish(device, arrived, project_weight, norm_gain):
    shapes = (((8, 3 * D), F32), ((8, 8, 128), F32), ((8, 1), F32))
    weight_rows = lax.dynamic_slice_in_dim(project_weight, 8 * device, 8, 0)
    gains = lax.dynamic_slice_in_dim(norm_gain, 8 * device, 8, 0)[:, None]
    return pl.pallas_call(
        finish_kernel,
        out_shape=[jax.ShapeDtypeStruct(*shape) for shape in shapes],
        in_specs=[VMEM] * 3,
        out_specs=[VMEM] * 3,
        compiler_params=pltpu.CompilerParams(vmem_limit_bytes=16 * 1024 * 1024),
        cost_estimate=pl.CostEstimate(flops=0, bytes_accessed=3_000_000, transcendentals=0),
        name="finish",
    )(arrived, weight_rows, gains)


def around(k):
    return [(i, (i // 4) * 4 + (i + k) % 4) for i in range(8)]


ACROSS = [(i, i ^ 4) for i in range(8)]
PARTNER = [(i, i ^ 1) for i in range(8)]


def gather_rows(mine):
    other = lax.ppermute(mine, "tx", ACROSS)
    pair = jnp.concatenate([mine, other], axis=0)
    return [pair] + [lax.ppermute(pair, "tx", around(k)) for k in (1, 2, 3)]


def gather_columns(mine):
    chunks = [mine] + [lax.ppermute(mine, "ty", shift(8, 2 * k)) for k in (1, 2, 3)]
    return [b for a in chunks for b in (a, lax.ppermute(a, "ty", PARTNER))]


def shards(
    velocity, viscosity, mean_flow, plane_pick, embed_weight, norm_gain, project_weight, output_weight, cotangent
):
    group, row, column = lax.axis_index("grp"), lax.axis_index("tx"), lax.axis_index("ty")

    device = (group * 8 + row) * 8 + column
    where = jnp.concatenate([group[None].astype(jnp.int32), plane_pick])
    flow = jnp.pad(mean_flow, 1)
    zhalo = lax.ppermute(pack_planes(velocity, viscosity), "grp", SWAP)
    there = pltpu.with_memory_space_constraint(viscosity, pltpu.HBM)
    heads, tails = pack_rows(velocity, there)
    xlow = lax.ppermute(tails, "tx", shift(8, 1))
    xhigh = lax.ppermute(heads, "tx", shift(8, -1))
    low, high = pack_columns(velocity, there, xlow, xhigh)
    low = lax.ppermute(low, "ty", shift(8, 1))
    high = lax.ppermute(high, "ty", shift(8, -1))
    edges = pack_edges(where, low, high, xlow, xhigh)
    zedge = lax.ppermute(edges, "grp", SWAP)
    halos = (zhalo, xlow, xhigh, edges[:TALL], zedge)
    kept, sent = sample_tokens(where, flow, velocity, viscosity, *halos)
    tokens = kept + lax.ppermute(sent, "grp", SWAP)
    cots = cotangent.reshape(128, D)
    weights = (embed_weight, project_weight, output_weight, norm_gain[None])
    column_part = layer(gather_columns(tokens), gather_columns(cots), *weights)
    cots = lax.optimization_barrier(cots)
    (partial,) = layer(gather_rows(tokens), gather_rows(cots), *weights, other=column_part)
    partial, late = lax.optimization_barrier((partial, where))
    new_velocity = stencil(late, flow, velocity, viscosity, *halos)
    arrived = lax.all_to_all(partial.reshape(128, 8, 512), ("grp", "tx", "ty"), split_axis=0, concat_axis=0, tiled=True)
    grad_project, pieces, grad_gain = finish(device, arrived, project_weight, norm_gain)
    pieces = lax.all_to_all(pieces, "tx", split_axis=0, concat_axis=0, tiled=True)
    grad_output = pieces.transpose(1, 0, 2).reshape(8, D)
    return new_velocity, grad_project, grad_output, grad_gain[:, 0]


def solution(mesh):
    in_specs = (
        P(None, "grp", "tx", "ty"),
        P("grp", "tx", "ty"),
        P(),
        P(),
        P(),
        P(),
        P(),
        P(),
        P("grp", "tx", "ty", None),
    )
    out_specs = (
        P(None, "grp", "tx", "ty"),
        P(("grp", "tx", "ty"), None),
        P(("grp", "tx", "ty"), None),
        P(("grp", "tx", "ty")),
    )

    return jax.shard_map(shards, mesh=mesh, in_specs=in_specs, out_specs=out_specs, check_vma=False)
```

```python
import functools

import jax
import jax.numpy as jnp
from jax import lax
from jax.experimental import pallas as pl
from jax.experimental.pallas import tpu as pltpu
from jax.sharding import PartitionSpec as P


D = 1024
CHANNELS = 3
HEAD_DIM = 64
PDIM = 768
DEPTH = 8
ROWS = 128
COLS = 256
NORM_EPS = 1e-06
F32 = jnp.float32
BF16 = jnp.bfloat16


TOP = 16
TALL = 160


def shift(count, step):
    return [(i, (i + step) % count) for i in range(count)]


SWAP = [(0, 1), (1, 0)]


VMEM = pl.BlockSpec(memory_space=pltpu.VMEM)
SMEM = pl.BlockSpec(memory_space=pltpu.SMEM)
ANY = pl.BlockSpec(memory_space=pl.ANY)
HBM = pl.BlockSpec(memory_space=pltpu.HBM)


NN = (((1,), (0,)), ((), ()))
NT = (((1,), (1,)), ((), ()))
TN = (((0,), (0,)), ((), ()))


def dot(a, b, dims=NN):
    return lax.dot_general(a, b, dims, preferred_element_type=F32)


def lane_ids(rows):
    return lax.broadcasted_iota(jnp.int32, (rows, 128), 1)


def beside(tiles, wanted, lane):
    forward = [pltpu.roll(tile, 127, 1) for tile in tiles]
    backward = [pltpu.roll(tile, 1, 1) for tile in tiles]
    following = [jnp.where(lane == 127, forward[(t + 1) % 3], forward[t]) for t in wanted]
    preceding = [jnp.where(lane == 0, backward[(t + 2) % 3], backward[t]) for t in wanted]
    return following, preceding


def substep_block(cells, plane, viscous, vplane, row, flow, lane, wanted):
    here = [viscous(vplane, t, row) for t in range(3)]
    following, preceding = beside(here, wanted, lane)
    faces, keep = [], []
    for t in wanted:
        sides = (
            viscous(vplane + 1, t, row),
            viscous(vplane - 1, t, row),
            viscous(vplane, t, row + 1),
            viscous(vplane, t, row - 1),
            following[t],
            preceding[t],
        )
        face = [here[t] + side for side in sides]
        keep.append(1.0 - (((face[0] + face[1]) + (face[2] + face[3])) + (face[4] + face[5])))
        face[2] = face[2] - flow
        face[3] = face[3] + flow
        faces.append(face)
    results = []
    for f in range(CHANNELS):
        centre = [cells(f, plane, t, row) for t in range(3)]
        following, preceding = beside(centre, wanted, lane)
        for t in wanted:
            face = faces[t]
            total = keep[t] * centre[t] + face[0] * cells(f, plane + 1, t, row)
            total = total + face[1] * cells(f, plane - 1, t, row)
            total = total + face[2] * cells(f, plane, t, row + 1)
            total = total + face[3] * cells(f, plane, t, row - 1)
            total = total + face[4] * following[t]
            total = total + face[5] * preceding[t]
            results.append((f, t, total))
    return results


def edge_tile(packed, k, lane):
    turned = pltpu.roll(packed, lax.rem(126 - 4 * k + 128, 128), 1)
    return jnp.where((lane < 2) | (lane >= 126), turned, 0.0)


class Block:
    def __init__(self, where_ref, zhalo_ref, xlow_ref, xhigh_ref, packed_ref, zedge_ref):
        self.group = where_ref[0]
        self.first = self.group == 0
        self.zhalo, self.xlow, self.xhigh, self.packed, self.zedge = zhalo_ref, xlow_ref, xhigh_ref, packed_ref, zedge_ref

    def fill_own(self, pad_ref, slot, z, load):
        packed = self.packed[...].astype(F32)
        lane = lane_ids(TALL)
        for f in range(4):
            scale = 1.0 if f < CHANNELS else 0.25
            source = load(f) * scale if f == CHANNELS else load(f)
            low = self.xlow[f, z].astype(F32) * scale
            high = self.xhigh[f, z].astype(F32) * scale
            for t in range(2):
                lanes = slice(128 * t, 128 * t + 128)
                pad_ref[f, slot, t, TOP : TOP + ROWS, :] = source[:, lanes]
                pad_ref[f, slot, t, TOP - 2 : TOP, :] = low[:, lanes]
                pad_ref[f, slot, t, TOP + ROWS : TOP + ROWS + 2, :] = high[:, lanes]
            pad_ref[f, slot, 2] = edge_tile(packed, f * DEPTH + z, lane) * scale

    def fill_halo(self, pad_ref, slot, j):
        packed = self.zedge[:TALL].astype(F32)
        edges = self.zedge[TALL:].astype(F32)
        lane = lane_ids(TALL)
        facing = jnp.where(self.first, 0, DEPTH - 1)
        for f in range(4):
            scale = 1.0 if f < CHANNELS else 0.25
            for t in range(2):
                lanes = slice(128 * t, 128 * t + 128)
                at = 2 * f + t
                pad_ref[f, slot, t, TOP : TOP + ROWS, :] = self.zhalo[f, j, :, lanes].astype(F32) * scale
                pad_ref[f, slot, t, TOP - 1 : TOP, :] = edges[at : at + 1] * scale
                pad_ref[f, slot, t, TOP + ROWS : TOP + ROWS + 1, :] = edges[8 + at : 9 + at] * scale
            pad_ref[f, slot, 2] = edge_tile(packed, f * DEPTH + facing, lane) * scale

    def fill_zero(self, pad_ref, slot):
        for f in range(pad_ref.shape[0]):
            for t in range(3):
                pad_ref[f, slot, t] = jnp.zeros((TALL, 128), F32)


def first_pass(pad_ref, half_ref, slot, flow, rim=True):
    lane = lane_ids(8)
    cells = lambda f, z, t, r: pad_ref[f, z, t, r : r + 8, :]
    viscous = lambda z, t, r: pad_ref[3, z, t, r : r + 8, :]
    rows = range(TOP - 8, TOP + ROWS + 8, 8) if rim else range(TOP, TOP + ROWS, 8)
    for row in rows:
        for f, t, done in substep_block(cells, slot + 1, viscous, slot + 1, row, flow, lane, (0, 1, 2) if rim else (0, 1)):
            half_ref[f, slot, t, row : row + 8, :] = done


def second_pass(pad_ref, half_ref, slot, flow, store):
    lane = lane_ids(8)
    cells = lambda f, p, t, r: half_ref[f, p, t, r : r + 8, :]
    viscous = lambda p, t, r: pad_ref[3, p, t, r : r + 8, :]
    for row in range(0, ROWS, 8):
        for f, t, done in substep_block(cells, slot + 1, viscous, slot + 2, TOP + row, flow, lane, (0, 1)):
            store(f, slice(row, row + 8), slice(128 * t, 128 * t + 128), done)


def stencil_kernel(where_ref, flow_ref, vel_ref, visc_ref, *refs):
    block = Block(where_ref, *refs[:5])
    new_ref, pad_ref, half_ref = refs[5:]
    first, group = block.first, block.group

    def fill(z, carry):
        block.fill_own(pad_ref, z + 2, z, lambda f: vel_ref[f, z] if f < CHANNELS else visc_ref[z])
        return carry

    lax.fori_loop(0, DEPTH, fill, 0)
    base = jnp.where(first, 10, 0)
    for j in range(2):
        block.fill_halo(pad_ref, base + j, j)
        block.fill_zero(pad_ref, 10 - base + j)

    def first_step(step, carry):
        at = step + jnp.where(first, 1, 0)
        first_pass(pad_ref, half_ref, at, 0.25 * flow_ref[group * DEPTH + at])
        return carry

    lax.fori_loop(0, 9, first_step, 0)
    block.fill_zero(half_ref, jnp.where(first, 0, 9))

    def second_step(z, carry):
        def store(f, rows, lanes, value):
            new_ref[f, z, rows, lanes] = value

        second_pass(pad_ref, half_ref, z, 0.25 * flow_ref[group * DEPTH + z + 1], store)
        return carry

    lax.fori_loop(0, DEPTH, second_step, 0)


def reorder(count, inner):
    row = lax.broadcasted_iota(jnp.int32, (count, count), 0)
    column = lax.broadcasted_iota(jnp.int32, (count, count), 1)
    outer = count // inner
    return (column == row % outer * inner + row // outer).astype(BF16)


def patchify(plane_ref, stage_ref, write):
    piece = lane_ids(8) // 16
    spread = reorder(128, 16)
    for c in range(CHANNELS):
        for t in range(2):
            turned = dot(spread, plane_ref[c, t].astype(BF16))
            for u in range(2):
                lines = [turned[64 * u + 8 * i : 64 * u + 8 * i + 8] for i in range(8)]
                for s in (1, 2, 4):
                    lower = (piece // s) % 2 == 0
                    for i in range(8):
                        if i & s == 0:
                            a, b = lines[i], lines[i + s]
                            lines[i] = jnp.where(lower, a, pltpu.roll(b, 16 * s, 1))
                            lines[i + s] = jnp.where(lower, pltpu.roll(a, 128 - 16 * s, 1), b)
                for b in range(8):
                    stage_ref[2 * c + u, 64 * t + 8 * b : 64 * t + 8 * b + 8, :] = lines[b]
    gather = reorder(128, 8)
    for u in range(6):
        write(u, dot(gather, stage_ref[u].astype(BF16)).astype(BF16))


def sample_kernel(where_ref, flow_ref, vel_ref, visc_ref, *refs):
    block = Block(where_ref, *refs[:5])
    kept_ref, sent_ref, pad_ref, half_ref, plane_ref, stage_ref, token_ref = refs[5:]
    first, group = block.first, block.group

    def sample(s, carry):
        local = where_ref[1 + s] - group * DEPTH
        inside = (local >= 0) & (local < DEPTH)

        def write(value):
            @pl.when(s == group)
            def _():
                value(kept_ref)

            @pl.when(s != group)
            def _():
                value(sent_ref)

        def write_zeros(ref):
            ref[...] = jnp.zeros((128, PDIM), BF16)

        def write_patches(ref):
            for u in range(6):
                ref[:, 128 * u : 128 * u + 128] = token_ref[u]

        @pl.when(jnp.logical_not(inside))
        def _():
            write(write_zeros)

        @pl.when(inside)
        def _():
            def fill(slot, c):
                z = local + slot - 2
                own = (z >= 0) & (z < DEPTH)
                halo = (first & (z >= DEPTH)) | (jnp.logical_not(first) & (z < 0))
                nothing = jnp.logical_not(own | halo)

                @pl.when(own)
                def _():
                    block.fill_own(pad_ref, slot, z, lambda f: vel_ref[f, z] if f < CHANNELS else visc_ref[z])

                @pl.when(halo)
                def _():
                    block.fill_halo(pad_ref, slot, jnp.where(first, z - DEPTH, z + 2))

                @pl.when(nothing)
                def _():
                    block.fill_zero(pad_ref, slot)

                return c

            lax.fori_loop(0, 5, fill, 0)

            def first_step(step, c):
                slot = 2 * step
                z = local + slot - 1
                outside = (first & (z < 0)) | (jnp.logical_not(first) & (z >= DEPTH))

                @pl.when(outside)
                def _():
                    block.fill_zero(half_ref, slot)

                @pl.when(jnp.logical_not(outside))
                def _():
                    first_pass(pad_ref, half_ref, slot, 0.25 * flow_ref[group * DEPTH + z + 1], rim=False)

                return c

            lax.fori_loop(0, 2, first_step, 0)
            first_pass(pad_ref, half_ref, 1, 0.25 * flow_ref[group * DEPTH + local + 1])

            def store(f, rows, lanes, value):
                plane_ref[f, lanes.start // 128, rows, :] = value

            second_pass(pad_ref, half_ref, 0, 0.25 * flow_ref[group * DEPTH + local + 1], store)

            def hold(u, value):
                token_ref[u] = value

            patchify(plane_ref, stage_ref, hold)
            write(write_patches)

        return carry

    lax.fori_loop(0, 2, sample, 0)


def pack_planes_kernel(vel_ref, visc_ref, plane_ref, stage, sems):
    two = pl.ds((1 - lax.axis_index("grp")) * (DEPTH - 2), 2)
    sources = [vel_ref.at[f, two] for f in range(CHANNELS)] + [visc_ref.at[two]]
    copies = [pltpu.make_async_copy(source, stage.at[f], sems.at[f]) for f, source in enumerate(sources)]
    for copy in copies:
        copy.start()
    for f, copy in enumerate(copies):
        copy.wait()
        plane_ref[f] = stage[f].astype(BF16)


def pack_planes(velocity, viscosity):
    shape = jax.ShapeDtypeStruct((4, 2, ROWS, COLS), BF16)
    scratch = [pltpu.VMEM((4, 2, ROWS, COLS), F32), pltpu.SemaphoreType.DMA((4,))]
    return local_call(pack_planes_kernel, shape, [HBM] * 2, scratch, 2, 24)(velocity, viscosity)


def pack_rows_kernel(vel_head, vel_tail, visc_hbm, head_ref, tail_ref, visc_ref, sems):
    copies = [
        pltpu.make_async_copy(visc_hbm.at[:, pl.ds(at, 8)], visc_ref.at[i], sems.at[i])
        for i, at in enumerate((0, ROWS - 8))
    ]
    for copy in copies:
        copy.start()
    for f in range(CHANNELS):
        head_ref[f] = vel_head[f, :, :2].astype(BF16)
        tail_ref[f] = vel_tail[f, :, 6:].astype(BF16)
    for copy in copies:
        copy.wait()
    head_ref[CHANNELS] = visc_ref[0, :, :2].astype(BF16)
    tail_ref[CHANNELS] = visc_ref[1, :, 6:].astype(BF16)


def pack_rows(velocity, viscosity):
    block = lambda at: pl.BlockSpec((CHANNELS, DEPTH, 8, COLS), lambda i: (0, 0, at, 0))
    return pl.pallas_call(
        pack_rows_kernel,
        grid=(1,),
        out_shape=(jax.ShapeDtypeStruct((4, DEPTH, 2, COLS), BF16),) * 2,
        in_specs=[block(0), block(ROWS // 8 - 1), HBM],
        out_specs=(VMEM,) * 2,
        scratch_shapes=[pltpu.VMEM((2, DEPTH, 8, COLS), F32), pltpu.SemaphoreType.DMA((2,))],
        compiler_params=pltpu.CompilerParams(vmem_limit_bytes=24 * 1024 * 1024),
        cost_estimate=pl.CostEstimate(flops=0, bytes_accessed=3_000_000, transcendentals=0),
        name="pack_rows",
    )(velocity, velocity, viscosity)


def pack_columns_kernel(vel_ref, visc_hbm, xlow_ref, xhigh_ref, low_ref, high_ref, low_stage, high_stage, visc_ref, sem):
    copy = pltpu.make_async_copy(visc_hbm, visc_ref, sem)
    copy.start()
    low_stage[...] = jnp.zeros_like(low_stage)
    high_stage[...] = jnp.zeros_like(high_stage)

    def pack(rows, load, fields, low, high):
        lane = lane_ids(rows)
        for f in fields:
            for z in range(DEPTH):
                k = f * DEPTH + z
                pair = lane // 2
                low = jnp.where(pair == 2 * k, pltpu.roll(load(f, z, 1), (4 * k + 2) % 128, 1), low)
                high = jnp.where(pair == 2 * k + 1, pltpu.roll(load(f, z, 0), 4 * k + 2, 1), high)
        return low, high

    def inner(f, z, t):
        lanes = slice(128 * t, 128 * t + 128)
        return vel_ref[f, z, :, lanes] if f < CHANNELS else visc_ref[z, :, lanes]

    nothing = jnp.zeros((1, 128), F32)
    for at, halo_ref, row in ((TOP - 1, xlow_ref, 1), (TOP + ROWS, xhigh_ref, 0)):
        load = lambda f, z, t: halo_ref[f, z, :, 128 * t : 128 * t + 128].astype(F32)[row : row + 1]
        low_stage[at : at + 1], high_stage[at : at + 1] = pack(1, load, range(4), nothing, nothing)
    nothing = jnp.zeros((ROWS, 128), F32)
    low, high = pack(ROWS, inner, range(CHANNELS), nothing, nothing)
    copy.wait()
    rows = slice(TOP, TOP + ROWS)
    low_stage[rows], high_stage[rows] = pack(ROWS, inner, (CHANNELS,), low, high)
    low_ref[...] = low_stage[...].astype(BF16)
    high_ref[...] = high_stage[...].astype(BF16)


def pack_edges_kernel(where_ref, low_ref, high_ref, xlow_ref, xhigh_ref, edge_ref, stage):
    edge_ref[:TALL] = low_ref[...] + high_ref[...]
    facing = jnp.where(where_ref[0] == 0, DEPTH - 1, 0)
    for f in range(4):
        for t in range(2):
            lanes = slice(128 * t, 128 * t + 128)
            at = 2 * f + t
            stage[at : at + 1] = xlow_ref[f, facing].astype(F32)[1:2, lanes]
            stage[8 + at : 9 + at] = xhigh_ref[f, facing].astype(F32)[0:1, lanes]
    edge_ref[TALL:] = stage[...].astype(BF16)


def local_call(kernel, out_shape, in_specs, scratch, us, mib, out_spec=VMEM):
    return pl.pallas_call(
        kernel,
        out_shape=out_shape,
        in_specs=in_specs,
        out_specs=jax.tree.map(lambda _: out_spec, out_shape),
        scratch_shapes=scratch,
        compiler_params=pltpu.CompilerParams(vmem_limit_bytes=mib * 1024 * 1024),
        cost_estimate=pl.CostEstimate(flops=0, bytes_accessed=us * 3_000_000, transcendentals=0),
    )


def stencil(*operands):
    scratch = [pltpu.VMEM((4, 12, 3, TALL, 128), F32), pltpu.VMEM((CHANNELS, 10, 3, TALL, 128), F32)]
    shape = jax.ShapeDtypeStruct((CHANNELS, DEPTH, ROWS, COLS), F32)
    return local_call(stencil_kernel, shape, [SMEM, SMEM] + [VMEM] * 7, scratch, 12, 48)(*operands)


def sample_tokens(*operands):
    scratch = [
        pltpu.VMEM((4, 5, 3, TALL, 128), F32),
        pltpu.VMEM((CHANNELS, 3, 3, TALL, 128), F32),
        pltpu.VMEM((CHANNELS, 2, ROWS, 128), F32),
        pltpu.VMEM((6, 128, 128), F32),
        pltpu.VMEM((6, 128, 128), BF16),
    ]
    shape = (jax.ShapeDtypeStruct((128, PDIM), BF16),) * 2
    specs = [SMEM, SMEM] + [VMEM] * 7
    return local_call(sample_kernel, shape, specs, scratch, 7, 32)(*operands)


def pack_columns(*operands):
    shape = (jax.ShapeDtypeStruct((TALL, 128), BF16),) * 2
    scratch = [pltpu.VMEM((TALL, 128), F32)] * 2 + [pltpu.VMEM((DEPTH, ROWS, COLS), F32), pltpu.SemaphoreType.DMA]
    return local_call(pack_columns_kernel, shape, [VMEM, HBM, VMEM, VMEM], scratch, 2, 24)(*operands)


def pack_edges(*operands):
    shape = jax.ShapeDtypeStruct((TALL + 16, 128), BF16)
    scratch = [pltpu.VMEM((16, 128), F32)]
    return local_call(pack_edges_kernel, shape, [SMEM] + [VMEM] * 4, scratch, 1, 24)(*operands)


def rounded(a):
    return a.astype(BF16).astype(F32)


def layer_kernel(along_rows, n_tokens, n_cots, *refs):
    n = n_tokens + n_cots
    embed_hbm, project_hbm, output_hbm, gain_hbm = refs[n : n + 4]
    other_hbm = refs[n + 4 : n + 6] if along_rows else ()
    outs = refs[n + 6 : n + 7] if along_rows else refs[n + 4 : n + 6]
    (
        tokens, cots, normed, qk, vg, weight, emb_even, emb_odd, rows_even, rows_odd, embed_ref, pair_ref, back_ref,
        gain_ref, sems, out_sems, *staged,
    ) = refs[n + 4 + len(other_hbm) + len(outs) :]
    head = lax.axis_index("tx") if along_rows else 8 + lax.axis_index("ty")
    started = []

    def start(source, target):
        started.append(pltpu.make_async_copy(source, target, sems.at[len(started)]))
        started[-1].start()

    for part in range(3):
        columns = pl.ds(pl.multiple_of(part * D + (head // 2) * 128, 128), 128)
        start(project_hbm.at[:, columns], pair_ref.at[part])
    start(embed_hbm, embed_ref)
    first_token = len(started)
    at = 0
    for piece in refs[:n_tokens]:
        start(piece, tokens.at[pl.ds(at, piece.shape[0])])
        at += piece.shape[0]
    start(gain_hbm, gain_ref)
    start(output_hbm.at[pl.ds(pl.multiple_of(head * HEAD_DIM, HEAD_DIM), HEAD_DIM)], back_ref)
    first_cot = len(started)
    at = 0
    for piece in refs[n_tokens:n]:
        start(piece, cots.at[pl.ds(at, piece.shape[0])])
        at += piece.shape[0]
    last = len(started)
    for source, target in zip(other_hbm, staged):
        start(source, target)
    lane = lane_ids(128)
    low = lane < 64

    def choose(is_odd):
        def rows(c, carry):
            at = pl.ds(pl.multiple_of(c * 128, 128), 128)
            query, key, value = (pair_ref[part, at, :].astype(F32) for part in range(3))
            turn = lambda a: pltpu.roll(a, 64, 1)
            query, key, value = (turn(query), key, turn(value)) if is_odd else (query, turn(key), value)
            weight[at, :128] = jnp.where(low, query, key).astype(BF16)
            weight[at, 128:] = jnp.where(low, value, 0.0).astype(BF16)
            return carry

        lax.fori_loop(0, 8, rows, 0)

    def chunk(c):
        return pl.ds(pl.multiple_of(lax.rem(c, 4) * 256, 256), 256)

    def embed(c, emb):
        emb[...] = dot(tokens[chunk(c), :], embed_ref[...]).astype(BF16)

    def normalise(c, emb, rows_ref):
        embedded = emb[...].astype(F32)
        centred = embedded - jnp.mean(embedded, axis=-1, keepdims=True)
        unit = centred * lax.rsqrt(jnp.mean(centred * centred, axis=-1, keepdims=True) + NORM_EPS)
        rows = (unit * gain_ref[...]).astype(BF16)
        rows_ref[...] = rows
        normed[chunk(c), :] = rows

    sorted_rows = (lambda a: dot(reorder(256, 16), a.astype(BF16))) if along_rows else (lambda a: a)

    def project(c, rows_ref):
        keep = lane_ids(256) < 64
        projected = rounded(dot(rows_ref[...], weight[...]))
        back = rounded(dot(cots[chunk(c), :], back_ref[...], NT))
        values = jnp.where(keep, projected[:, 128:], jnp.concatenate([back, back], axis=1))
        if along_rows:
            both = sorted_rows(jnp.concatenate([projected[:, :128], values], axis=1))
            qk[chunk(c), :] = both[:, :128]
            vg[chunk(c), :] = both[:, 128:]
        else:
            qk[chunk(c), :] = projected[:, :128]
            vg[chunk(c), :] = values

    def landed(pieces, count, whole, base, c):
        rows = 1024 // count
        for k in range(count // 4):
            piece = count // 4 * c + k
            target = whole.at[pl.ds(pl.multiple_of(piece * rows, rows), rows)]
            pltpu.make_async_copy(pieces[0], target, sems.at[base + piece]).wait()

    token_landed = lambda c: landed(refs[:n_tokens], n_tokens, tokens, first_token, c)
    cot_landed = lambda c: landed(refs[n_tokens:n], n_cots, cots, first_cot, c)
    for copy in started[:3]:
        copy.wait()
    odd = lax.rem(head, 2) == 1

    @pl.when(odd)
    def _():
        choose(True)

    @pl.when(jnp.logical_not(odd))
    def _():
        choose(False)

    started[3].wait()
    token_landed(0)
    embed(0, emb_even)
    for copy in started[first_cot - 2 : first_cot]:
        copy.wait()

    def step(i, carry):
        c = 2 * i
        token_landed(c + 1)

        @pl.when(i == 0)
        def _():
            token_landed(2)

        cot_landed(c)
        cot_landed(c + 1)
        embed(c + 1, emb_odd)
        normalise(c, emb_even, rows_even)
        project(jnp.maximum(c - 1, 0), rows_odd)
        embed(c + 2, emb_even)
        normalise(c + 1, emb_odd, rows_odd)
        project(c, rows_even)
        return carry

    lax.fori_loop(0, 2, step, 0)
    project(3, rows_odd)
    if along_rows:
        row = lax.broadcasted_iota(jnp.int32, (128, 128), 0)
        same = (row // 16) % 2 == (lane // 16) % 2
        spots = lambda p: [256 * c + 32 * p for c in range(4)]
        size = 32
    else:
        spots = lambda p: [128 * c + 16 * p for c in range(8)]
        size = 16
    only_low = lambda a: jnp.where(low, a, 0.0).astype(BF16)
    only_high = lambda a: jnp.where(low, 0.0, a).astype(BF16)

    def load(ref, p):
        return jnp.concatenate([ref[at : at + size, :] for at in spots(p)], axis=0)

    def store(ref, p, value):
        for k, at in enumerate(spots(p)):
            ref[at : at + size, :] = value[size * k : size * k + size]

    for first in range(0, 8, 4):
        blocks = range(first, first + 4)
        wide = [(load(qk, p), load(vg, p)) for p in blocks]
        turned = [(pltpu.roll(a, 64, 1), pltpu.roll(b, 64, 1)) for a, b in wide]
        scores = [dot(only_low(a), t.astype(BF16), NT) * HEAD_DIM**-0.5 for (a, _), (t, _) in zip(wide, turned)]
        dprobs = [dot(only_low(t), b.astype(BF16), NT) for (_, b), (_, t) in zip(wide, turned)]
        if along_rows:
            scores = [jnp.where(same, a, -1e30) for a in scores]
        raised = [jnp.exp(a - jnp.max(a, axis=-1, keepdims=True)) for a in scores]
        probs = [a / jnp.sum(a, axis=-1, keepdims=True) for a in raised]
        deltas = [jnp.sum(a * d, axis=-1, keepdims=True) for a, d in zip(probs, dprobs)]
        weights = [a.astype(BF16) for a in probs]
        dscores = [(a * (d - e) * HEAD_DIM**-0.5).astype(BF16) for a, d, e in zip(probs, dprobs, deltas)]
        dqk = [dot(d, only_low(t)) + dot(d, only_high(t), TN) for d, (t, _) in zip(dscores, turned)]
        dva = [dot(w, only_low(t), TN) + dot(w, only_high(t)) for w, (_, t) in zip(weights, turned)]
        for p, a, b in zip(blocks, dqk, dva):
            store(qk, p, a)
            store(vg, p, b)
    both = jnp.concatenate([qk[...].astype(BF16), vg[...].astype(BF16)], axis=1)
    if along_rows:
        unsort = reorder(256, 16)
        both = jnp.concatenate([dot(unsort, both[256 * c : 256 * c + 256]).astype(BF16) for c in range(4)], axis=0)
    grad_output = dot(both[:, 128:], cots[...], TN)[64:]
    grad_project = dot(normed[...], both, TN)
    if not along_rows:
        other_project, other_output = staged
        other_output[...] = grad_output
        other_project[...] = grad_project.astype(BF16)
        sent = [
            pltpu.make_async_copy(source, target, out_sems.at[i])
            for i, (source, target) in enumerate(zip(staged, outs))
        ]
        for copy in sent:
            copy.start()
        for copy in sent:
            copy.wait()
        return
    for copy in started[last:]:
        copy.wait()
    low64 = lane_ids(64) < 64
    other_project, other_output, whole = staged
    sent = []
    for c in range(16):
        rows = slice(64 * c, 64 * c + 64)
        lanes = slice(128 * (c % 8), 128 * (c % 8) + 128)
        piece = grad_output[:, lanes] if c < 8 else other_output[:, lanes]
        whole[rows, :128] = grad_project[rows, :128].astype(BF16)
        whole[rows, 128:256] = jnp.where(low64, grad_project[rows, 128:], pltpu.roll(piece, 64, 1)).astype(BF16)
        whole[rows, 256:384] = other_project[rows, :128]
        whole[rows, 384:] = jnp.where(low64, other_project[rows, 128:].astype(F32), piece).astype(BF16)
        if c % 4 == 3:
            quarter = pl.ds(64 * (c - 3), 256)
            sent.append(pltpu.make_async_copy(whole.at[quarter], outs[0].at[quarter], out_sems.at[c // 4]))
            sent[-1].start()
    for copy in sent:
        copy.wait()


def layer(tokens, cots, embed_weight, project_weight, output_weight, gain, other=None):
    along_rows = other is not None
    kernel = functools.partial(layer_kernel, along_rows, len(tokens), len(cots))
    shapes = (((D, 512), BF16),) if along_rows else (((D, 256), BF16), ((HEAD_DIM, D), F32))
    operands = [*tokens, *cots, embed_weight, project_weight, output_weight]
    others = (gain,) + (other or ())
    chunk = [pltpu.VMEM((256, D), BF16)] * 4
    scratch = [
        pltpu.VMEM((1024, PDIM), BF16),
        pltpu.VMEM((1024, D), BF16),
        pltpu.VMEM((1024, D), BF16),
        pltpu.VMEM((1024, 128), F32),
        pltpu.VMEM((1024, 128), F32),
        pltpu.VMEM((D, 256), BF16),
        *chunk,
        pltpu.VMEM((PDIM, D), BF16),
        pltpu.VMEM((3, D, 128), BF16),
        pltpu.VMEM((HEAD_DIM, D), BF16),
        pltpu.VMEM((1, D), F32),
        pltpu.SemaphoreType.DMA((len(operands) + 5,)),
        pltpu.SemaphoreType.DMA((4,)),
        pltpu.VMEM((D, 256), BF16),
        pltpu.VMEM((HEAD_DIM, D), F32),
    ]
    if along_rows:
        scratch.append(pltpu.VMEM((D, 512), BF16))
    return local_call(
        kernel,
        tuple(jax.ShapeDtypeStruct(*shape) for shape in shapes),
        [ANY] * (len(operands) + len(others)),
        scratch,
        11,
        60,
        HBM,
    )(*operands, *others)


def total(arrived_ref, head, tile, along_rows):
    spots = [(g, head, m) if along_rows else (g, m, head) for g in range(2) for m in range(8)]
    values = [
        arrived_ref[64 * g + 8 * x + y, :, 128 * tile : 128 * tile + 128].astype(F32) for g, x, y in spots
    ]
    while len(values) > 1:
        values = [a + b for a, b in zip(values[::2], values[1::2])]
    return values[0]


def pieces_kernel(one_ref, two_ref, piece_ref):
    low = lane_ids(8) < 64
    first = lax.axis_index("grp") == 0
    for along_rows in (True, False):

        @pl.when(first if along_rows else jnp.logical_not(first))
        def _():
            for h in range(8):
                one, two = (total(ref, h, 0, along_rows) for ref in (one_ref, two_ref))
                piece_ref[h] = jnp.where(low, pltpu.roll(one, 64, 1), two)


def finish_kernel(arrived_ref, weight_ref, gain_ref, project_ref, norm_ref):
    low = lane_ids(8) < 64
    turn = lambda a: pltpu.roll(a, 64, 1)
    gain_total = jnp.zeros((8, 128), F32)
    for along_rows in (True, False):
        tile = 0 if along_rows else 2
        for m in range(4):
            (qk_even, v_even), (qk_odd, v_odd) = (
                [total(arrived_ref, h, tile + k, along_rows) for k in range(2)] for h in (2 * m, 2 * m + 1)
            )
            columns = (
                jnp.where(low, qk_even, turn(qk_odd)),
                jnp.where(low, turn(qk_even), qk_odd),
                jnp.where(low, v_even, turn(v_odd)),
            )
            for k, value in enumerate(columns):
                at = D * k + 128 * m + (0 if along_rows else 512)
                project_ref[:, at : at + 128] = value
                gain_total = gain_total + weight_ref[:, at : at + 128].astype(F32) * value
    norm_ref[...] = jnp.sum(gain_total, axis=1, keepdims=True) / gain_ref[...]


def pieces(arrived):
    shape = jax.ShapeDtypeStruct((8, 8, 128), F32)
    return pl.pallas_call(
        pieces_kernel,
        grid=(1,),
        out_shape=shape,
        in_specs=[pl.BlockSpec((128, 8, 128), lambda i: (0, 0, 1)), pl.BlockSpec((128, 8, 128), lambda i: (0, 0, 3))],
        out_specs=VMEM,
        compiler_params=pltpu.CompilerParams(vmem_limit_bytes=16 * 1024 * 1024),
        cost_estimate=pl.CostEstimate(flops=0, bytes_accessed=3_000_000, transcendentals=0),
        name="pieces",
    )(arrived, arrived)


def finish(device, arrived, project_weight, norm_gain):
    shapes = (jax.ShapeDtypeStruct((8, 3 * D), F32), jax.ShapeDtypeStruct((8, 1), F32))
    weight_rows = lax.dynamic_slice_in_dim(project_weight, 8 * device, 8, 0)
    gains = lax.dynamic_slice_in_dim(norm_gain, 8 * device, 8, 0)[:, None]
    return local_call(finish_kernel, shapes, [VMEM] * 3, [], 2, 16)(arrived, weight_rows, gains)


def around(k):
    return [(i, (i // 4) * 4 + (i + k) % 4) for i in range(8)]


ACROSS = [(i, i ^ 4) for i in range(8)]
PARTNER = [(i, i ^ 1) for i in range(8)]


def gather_rows(mine):
    other = lax.ppermute(mine, "tx", ACROSS)
    pair = jnp.concatenate([mine, other], axis=0)
    return [pair] + [lax.ppermute(pair, "tx", around(k)) for k in (1, 2, 3)]


def gather_columns(mine):
    chunks = [mine] + [lax.ppermute(mine, "ty", shift(8, 2 * k)) for k in (1, 2, 3)]
    return [b for a in chunks for b in (a, lax.ppermute(a, "ty", PARTNER))]


def shards(
    velocity, viscosity, mean_flow, plane_pick, embed_weight, norm_gain, project_weight, output_weight, cotangent
):
    group, row, column = lax.axis_index("grp"), lax.axis_index("tx"), lax.axis_index("ty")

    device = (group * 8 + row) * 8 + column
    where = jnp.concatenate([group[None].astype(jnp.int32), plane_pick])
    flow = jnp.pad(mean_flow, 1)
    there = pltpu.with_memory_space_constraint(viscosity, pltpu.HBM)
    far = pltpu.with_memory_space_constraint(velocity, pltpu.HBM)
    zhalo = lax.ppermute(pack_planes(far, there), "grp", SWAP)
    heads, tails = pack_rows(velocity, there)
    xlow = lax.ppermute(tails, "tx", shift(8, 1))
    xhigh = lax.ppermute(heads, "tx", shift(8, -1))
    low, high = pack_columns(velocity, there, xlow, xhigh)
    low = lax.ppermute(low, "ty", shift(8, 1))
    high = lax.ppermute(high, "ty", shift(8, -1))
    edges = pack_edges(where, low, high, xlow, xhigh)
    zedge = lax.ppermute(edges, "grp", SWAP)
    halos = (zhalo, xlow, xhigh, edges[:TALL], zedge)
    kept, sent = sample_tokens(where, flow, velocity, viscosity, *halos)
    tokens = kept + lax.ppermute(sent, "grp", SWAP)
    cots = cotangent.reshape(128, D)
    weights = (embed_weight, project_weight, output_weight, norm_gain[None])
    column_part = layer(gather_columns(tokens), gather_columns(cots), *weights)
    cots = lax.optimization_barrier(cots)
    (partial,) = layer(gather_rows(tokens), gather_rows(cots), *weights, other=column_part)
    partial, late = lax.optimization_barrier((partial, where))
    new_velocity = stencil(late, flow, velocity, viscosity, *halos)
    arrived = lax.all_to_all(partial.reshape(128, 8, 512), ("grp", "tx", "ty"), split_axis=0, concat_axis=0, tiled=True)
    exchanged = lax.all_to_all(pieces(arrived), "tx", split_axis=0, concat_axis=0, tiled=True)
    grad_project, grad_gain = finish(device, arrived, project_weight, norm_gain)
    grad_output = exchanged.transpose(1, 0, 2).reshape(8, D)
    return new_velocity, grad_project, grad_output, grad_gain[:, 0]


def solution(mesh):
    in_specs = (
        P(None, "grp", "tx", "ty"),
        P("grp", "tx", "ty"),
        P(),
        P(),
        P(),
        P(),
        P(),
        P(),
        P("grp", "tx", "ty", None),
    )
    out_specs = (
        P(None, "grp", "tx", "ty"),
        P(("grp", "tx", "ty"), None),
        P(("grp", "tx", "ty"), None),
        P(("grp", "tx", "ty")),
    )

    return jax.shard_map(shards, mesh=mesh, in_specs=in_specs, out_specs=out_specs, check_vma=False)
```
